32 devices in a mesh: vessel: 8 (over y, x, core), xsec: 4 (over z).
Axes of the slice: x: 2, y: 2, z: 4, core: 2. Of those that a mesh axis runs over, the one named last changes fastest.
Arguments:
- populations: float32 [19, 256, 2048], P(None, 'vessel', 'xsec'), may hold values from 0 to 1, as said below
- wall_flags: int32 [256, 2048], P('vessel', 'xsec'), may hold values from 0 to 1, as said below
- positions: float32 [256, 3, 128], P(('vessel', 'xsec')), may hold values from 0 to 31, as said below
- vertex_rest_shift: float32 [256, 3, 128], P(('vessel', 'xsec')), may hold values from -3 to 3
- home_brick: int32 [256, 1], P(('vessel', 'xsec')), may hold values from 0 to 3; in each aligned block of 8 rows (0 to 7, 8 to 15, ...) at most 4 rows name the same one
Outputs:
- evolved: float32 [19, 256, 2048], P(None, 'vessel', 'xsec')
- displacement: float32 [256, 3, 128], P(('vessel', 'xsec'))
The draws below stay inside these ranges and needn't reach their ends.
Inputs may be any that keep to these rules, and one draw needn't show every extreme that they name: `home_brick`: within the 8 blocks of one device no home index occurs more than 4 times. `positions`: the first coordinate lies within 0 to 31, the second within 0 to 15, the third within 0 to 31. `wall_flags`: every cell with y = 0, y = 63, z = 0 or z = 31 is a wall. `populations`: all entries are positive.
All inputs are finite; a program needn't handle non-finite values.
Results may differ from the reference program's by a relative error of at most 0.0033.
Values sent between devices are 32-bit elements; how exact they have to be, the bound alone decides.
A program may use at most 64 MiB of HBM per device.

```python
import math
import jax
import jax.numpy as jnp
import numpy as np
from jax import lax

Q = 19
NY = 64
NZ = 32
CX = 32
NBLK = 8
B = 128
ITERS = 2
CY = 16
CAP = 4
NX = 256
NBLOCKS = 256
N_VESSEL = 8
N_XSEC = 4


WEIGHTS = [1.0 / 3.0] + [1.0 / 18.0] * 6 + [1.0 / 36.0] * 12


def draw_populations(key, part):
    weights = jnp.asarray(WEIGHTS, jnp.float32)[:, None, None]
    factor = jax.random.uniform(key, (Q, NX, NY * NZ), jnp.float32, 0.7, 1.3)
    return weights * factor


def draw_positions(key, part):
    key_centre, key_points = jax.random.split(key)
    extent = jnp.asarray([CX, CY, NZ], jnp.float32)[None, :, None]
    centre = extent * (0.3 + 0.4 * jax.random.uniform(key_centre, (NBLOCKS, 3, 1), jnp.float32)) - 0.5
    spread = jnp.minimum(1.5, extent / 6.0)
    points = centre + spread * jax.random.normal(key_points, (NBLOCKS, 3, B), jnp.float32)
    return jnp.clip(points, 0.0, extent - 1.0)


def draw_wall_flags(key, part):
    rows_x = jnp.arange(NX, dtype=jnp.int32)[:, None]
    flat_index = jnp.arange(NY * NZ, dtype=jnp.int32)[None, :]
    across = flat_index // NZ
    depth_index = flat_index % NZ
    border = (across == 0) | (across == NY - 1) | (depth_index == 0) | (depth_index == NZ - 1)
    septum = ((across == NY // 2) | (across == NY // 2 - 1)) & (rows_x % (2 * CX) >= CX)
    septum = septum & (depth_index >= NZ // 4) & (depth_index < 3 * NZ // 4)
    sparse = jax.random.randint(key, (NX, NY * NZ), 0, 48) == 0
    return (border | septum | sparse).astype(jnp.int32)


def block_levels(stream_key, shape, shards, low, high):
    def one(dim, blocks):
        draws = jax.random.uniform(jax.random.fold_in(jax.random.fold_in(stream_key, 6), dim), (blocks,), jnp.float32, low / len(shards), high / len(shards))
        return jnp.repeat(jnp.exp(draws), shape[dim] // blocks).reshape((-1,) + (1,) * (len(shape) - dim - 1))

    factor_of = one(*shards[0])
    for cut in shards[1:]:
        factor_of = factor_of * one(*cut)
    return factor_of


def assign_block(own_key, own, number, rows, number_of, top, reach, skew):
    order = jax.random.permutation(own_key, number_of)
    heavy_load, usual = load_shares(number_of, rows * top, reach, skew, True), load_shares(number_of, rows * top, reach, skew, False)
    places = jnp.arange(number_of)

    def named(sizes, turn):
        used = int((sizes > 0).sum())
        fixed = max(1, used // 4)
        moved = fixed + (places - fixed + turn * (used - fixed)) % max(1, number_of - fixed)
        return jnp.zeros((number_of,), jnp.int32).at[order[jnp.where(places < fixed, places, moved)]].set(jnp.asarray(sizes, jnp.int32))

    sizes = jnp.where(number % 4 == 0, named(heavy_load, number // 4), named(usual, number - number // 4 - 1))
    mixed = jax.random.permutation(jax.random.fold_in(own, 3), number_of)
    donor, sink = mixed[0:number_of // 2 * 2:2], mixed[1:number_of // 2 * 2:2]
    room = jnp.minimum(sizes[donor] - 1, reach - sizes[sink]) // 2
    room = jnp.where((donor == order[0]) | (sink == order[0]) | (sizes[sink] == 0), 0, jnp.maximum(room, 0))
    moved = jax.random.randint(jax.random.fold_in(own, 4), (number_of // 2,), 0, 1 << 20) % (room + 1)
    sizes = sizes.at[donor].add(-moved).at[sink].add(moved)
    members = jnp.searchsorted(jnp.cumsum(sizes), jnp.arange(rows * top), side="right").astype(jnp.int32)
    grid = members.reshape(top, rows).T
    grid = grid[jax.random.permutation(jax.random.fold_in(own, 1), rows)]
    turn = jax.random.randint(jax.random.fold_in(own, 2), (rows, 1), 0, top)
    return jnp.take_along_axis(grid, (jnp.arange(top)[None, :] + turn) % top, axis=1)


def load_shares(number_of, total, most, lean, full):
    weights = [(1 << 20) // math.isqrt(rank ** lean) + 1 for rank in range(1, number_of + 1)]
    largest = most if full else min(most, max(-(-total // number_of), total * weights[0] // sum(weights)))
    least = 1 if total - largest >= number_of - 1 else 0
    given, spare = [largest] + [least] * (number_of - 1), total - largest - least * (number_of - 1)
    while spare > 0:
        movable = [i for i in range(1, number_of) if given[i] < largest] or [i for i in range(1, number_of) if given[i] < most]
        mass, remaining = sum([weights[i] for i in movable]), spare
        for i in movable:
            addition = min(most - given[i], max(1, remaining * weights[i] // mass), spare)
            given[i] = given[i] + addition
            spare = spare - addition
    return np.array(given)


def bell_draw(rng, dims, scale, most, cuts=(), held_as=jnp.bfloat16):
    factor_of = block_levels(rng, dims, cuts, -0.22, 0.18) if cuts else 1.0
    result = jax.random.normal(rng, dims, jnp.float32) * scale * factor_of
    return jnp.minimum(jnp.maximum(result, -most), most).astype(held_as)


def setup_inputs(seed: int = 0) -> dict:
    seeds = jax.random.split(jax.random.key(seed), 6)
    populations = draw_populations(jax.random.fold_in(seeds[5], 71), 0)
    wall_flags = draw_wall_flags(jax.random.fold_in(seeds[5], 71), 0)
    positions = draw_positions(jax.random.fold_in(seeds[5], 71), 0)
    vertex_rest_shift = bell_draw(seeds[3], (NBLOCKS, 3, B), 0.7, 3.0, ((0, 32),), jnp.float32)
    home_brick_keys = jax.random.split(jax.random.fold_in(seeds[4], 1), NBLOCKS // NBLK)
    home_brick_turns = jax.random.permutation(jax.random.fold_in(seeds[4], 3), NBLOCKS // NBLK)
    home_brick = jax.vmap(lambda own, number: assign_block(jax.random.fold_in(seeds[4], 2), own, number, NBLK, N_XSEC, 1, CAP, 2))(home_brick_keys, home_brick_turns).reshape((NBLOCKS, 1))
    return dict(populations=populations, wall_flags=wall_flags, positions=positions, vertex_rest_shift=vertex_rest_shift, home_brick=home_brick)


LATTICE = [[0, 0, 0], [1, 0, 0], [-1, 0, 0], [0, 1, 0], [0, -1, 0], [0, 0, 1], [0, 0, -1],
           [1, 1, 0], [-1, -1, 0], [1, -1, 0], [-1, 1, 0], [1, 0, 1], [-1, 0, -1], [1, 0, -1],
           [-1, 0, 1], [0, 1, 1], [0, -1, -1], [0, 1, -1], [0, -1, 1]]
OPPOSITE = [0, 2, 1, 4, 3, 6, 5, 8, 7, 10, 9, 12, 11, 14, 13, 16, 15, 18, 17]
WEIGHTS = [1.0 / 3.0] + [1.0 / 18.0] * 6 + [1.0 / 36.0] * 12
RELAX_TIME = 0.8
SPRING = 0.1
TOP_PRECISION = lax.Precision.HIGHEST


def collide(populations, wall_flags, force_field):
    lattice = jnp.asarray(LATTICE, jnp.float32)
    weights = jnp.asarray(WEIGHTS, jnp.float32)[:, None, None]
    density = jnp.sum(populations, axis=0)
    momentum = jnp.tensordot(lattice.T, populations, axes=1, precision=TOP_PRECISION)
    shifted = (momentum + RELAX_TIME * force_field) / density
    project = jnp.tensordot(lattice, shifted, axes=1, precision=TOP_PRECISION)
    square = jnp.sum(shifted * shifted, axis=0)
    balance = weights * density * (1.0 + 3.0 * project + 4.5 * project * project - 1.5 * square)
    relaxed = populations - (populations - balance) / RELAX_TIME
    bounced = jnp.stack([populations[member] for member in OPPOSITE])
    return jnp.where(wall_flags[None] == 1, bounced, relaxed)


def fluid_velocity(populations, force_field):
    lattice = jnp.asarray(LATTICE, jnp.float32)
    density = jnp.sum(populations, axis=0)
    momentum = jnp.tensordot(lattice.T, populations, axes=1, precision=TOP_PRECISION)
    return ((momentum + 0.5 * force_field) / density).astype(jnp.bfloat16)


def hat_weights(coordinate, extent):
    centres = jnp.arange(extent, dtype=jnp.float32)
    return jnp.maximum(0.0, 1.0 - jnp.abs(coordinate[..., None] - centres))


def kernel_weights(points, extent_x, extent_y, depth_cells):
    weight_x = hat_weights(points[:, 0], extent_x)
    weight_y = hat_weights(points[:, 1], extent_y)
    weight_z = hat_weights(points[:, 2], depth_cells)
    weight_yz = weight_y[:, :, :, None] * weight_z[:, :, None, :]
    shape_out = (points.shape[0], points.shape[2], extent_y * depth_cells)
    return weight_x, weight_yz.reshape(shape_out).astype(jnp.bfloat16)


def stream_grid(relaxed):
    lattice_grid = relaxed.reshape(len(LATTICE), NX, NY, NZ)
    pieces = []
    for direction in range(len(LATTICE)):
        step_x, step_y, step_z = LATTICE[direction]
        rolled = jnp.roll(lattice_grid[direction], step_x, axis=0)
        padded_rows = jnp.pad(rolled, ((0, 0), (1, 1), (1, 1)))
        pieces.append(padded_rows[:, 1 - step_y:1 - step_y + NY, 1 - step_z:1 - step_z + NZ])
    return jnp.stack(pieces).reshape(len(LATTICE), NX, NY * NZ)


def reference(populations, wall_flags, positions, vertex_rest_shift, home_brick):
    group_size = N_XSEC * NBLK
    plane_cells = CY * NZ
    anchors = positions + vertex_rest_shift
    chooser_all = (home_brick[:, 0].reshape(N_VESSEL, group_size)[:, :, None]
                   == jnp.arange(N_XSEC, dtype=jnp.int32)).astype(jnp.float32)

    def spread_slab(inputs):
        points, forces, chooser = inputs
        weight_x, weight_yz = kernel_weights(points, CX, CY, NZ)
        left_side = (forces[:, :, None, :] * jnp.transpose(weight_x, (0, 2, 1))[:, None]).reshape(group_size, 3 * CX, B)
        left_side = lax.optimization_barrier(left_side.astype(jnp.bfloat16)).astype(jnp.float32)
        kernel_yz = lax.optimization_barrier(weight_yz).astype(jnp.float32)
        pieces = jnp.einsum("gkb,gbn->gkn", left_side, kernel_yz, precision=TOP_PRECISION)
        return jnp.einsum("gh,gkn->khn", chooser, pieces, precision=TOP_PRECISION)

    def read_slab(inputs):
        points, bricks, chooser = inputs
        weight_x, weight_yz = kernel_weights(points, CX, CY, NZ)
        kernel_yz = lax.optimization_barrier(weight_yz).astype(jnp.float32)
        bricks_wide = lax.optimization_barrier(bricks).astype(jnp.float32)
        picked = jnp.einsum("gh,hkn->gkn", chooser, bricks_wide, precision=TOP_PRECISION)
        sampled = jnp.einsum("gkn,gbn->gkb", picked, kernel_yz, precision=TOP_PRECISION).reshape(group_size, 3, CX, B)
        return jnp.sum(sampled * jnp.transpose(weight_x, (0, 2, 1))[:, None], axis=2)

    present_state = positions
    lattice_state = populations
    for iteration in range(ITERS):
        forces = SPRING * (anchors - present_state)
        blocks_now = present_state.reshape(N_VESSEL, group_size, 3, B)
        slab_fields = lax.map(spread_slab, (blocks_now, forces.reshape(N_VESSEL, group_size, 3, B), chooser_all))
        force_field = slab_fields.reshape(N_VESSEL, 3, CX, N_XSEC * plane_cells)
        force_field = force_field.transpose(1, 0, 2, 3).reshape(3, NX, NY * NZ)
        lattice_state = stream_grid(collide(lattice_state, wall_flags, force_field))
        velocity = fluid_velocity(lattice_state, force_field)
        bricks = velocity.reshape(3, N_VESSEL, CX, N_XSEC, plane_cells).transpose(1, 3, 0, 2, 4)
        bricks = bricks.reshape(N_VESSEL, N_XSEC, 3 * CX, plane_cells)
        travel = lax.map(read_slab, (blocks_now, bricks, chooser_all))
        present_state = present_state + travel.reshape(NBLOCKS, 3, B)
    return lattice_state, present_state - positions
```

```python
import functools

import jax
import jax.numpy as jnp
from jax import lax
from jax.experimental import pallas as pl
from jax.experimental.pallas import tpu as pltpu
from jax.sharding import PartitionSpec as P

NZ = 32
ITERS = 2
LATTICE = [
    [0, 0, 0],
    [1, 0, 0],
    [-1, 0, 0],
    [0, 1, 0],
    [0, -1, 0],
    [0, 0, 1],
    [0, 0, -1],
    [1, 1, 0],
    [-1, -1, 0],
    [1, -1, 0],
    [-1, 1, 0],
    [1, 0, 1],
    [-1, 0, -1],
    [1, 0, -1],
    [-1, 0, 1],
    [0, 1, 1],
    [0, -1, -1],
    [0, 1, -1],
    [0, -1, 1],
]
Q = len(LATTICE)
OPPOSITE = [0, 2, 1, 4, 3, 6, 5, 8, 7, 10, 9, 12, 11, 14, 13, 16, 15, 18, 17]
WEIGHTS = [1.0 / 3.0] + [1.0 / 18.0] * 6 + [1.0 / 36.0] * 12
RELAX_TIME = 0.8
SPRING = 0.1
LANES = 128
GROUPS = LANES // NZ
MESH = pl.DeviceIdType.MESH
X_DIRS = {s: [q for q in range(Q) if LATTICE[q][0] == s] for s in (1, -1)}
Y_DIRS = {s: [q for q in range(Q) if LATTICE[q][1] == s] for s in (1, -1)}
CORNERS = [q for q in range(Q) if LATTICE[q][0] != 0 and LATTICE[q][1] != 0]


def signed_sum(terms):
    total = None
    for sign, value in terms:
        if total is None:
            total = value if sign > 0 else -value
        else:
            total = total + value if sign > 0 else total - value
    return total


def tree_sum(terms):
    while len(terms) > 1:
        terms = [
            terms[i] + terms[i + 1] if i + 1 < len(terms) else terms[i]
            for i in range(0, len(terms), 2)
        ]
    return terms[0]


def moments(fs):
    both = [fs[q] + fs[OPPOSITE[q]] for q in range(1, Q, 2)]
    flow = {q: fs[q] - fs[OPPOSITE[q]] for q in range(1, Q, 2)}
    density = tree_sum([fs[0]] + both)
    momentum = []
    for d in range(3):
        plus = tree_sum([flow[q] for q in flow if LATTICE[q][d] == 1])
        minus = [flow[q] for q in flow if LATTICE[q][d] == -1]
        momentum.append(plus - tree_sum(minus) if minus else plus)
    return density, momentum


def kernel(
    n_vessel, n_xsec, capacity, extent_x, plane,
    pop_hbm, wall_hbm, pos_hbm, shift_hbm, home_hbm, fbuf, disp,
    wall, pos, shift, home, rbuf, mom, force, vel,
    blocks, outgoing, arrived, current, ret_out, ret_in,
    xs_out, xs_in, ys_out, ys_in, cs_in,
    pop_sem, wall_sem, small_sem, a2a_send, a2a_recv, ret_send, ret_recv, halo_send, halo_recv,
):
    v = lax.axis_index("vessel")
    h = lax.axis_index("xsec")
    v_side = {1: lax.rem(v + 1, n_vessel), -1: lax.rem(v + n_vessel - 1, n_vessel)}
    owned = pos.shape[1]
    slots = n_xsec * capacity
    extent_y = plane // NZ
    tiles = plane // LANES
    row_groups = extent_x // 8

    small_loads = [
        pltpu.make_async_copy(source, target, small_sem.at[i])
        for i, (source, target) in enumerate(
            ((pos_hbm, pos), (shift_hbm, shift), (home_hbm, home))
        )
    ]
    for copy in small_loads:
        copy.start()
    load = pltpu.make_async_copy(pop_hbm, fbuf, pop_sem)
    load.start()
    load_wall = pltpu.make_async_copy(wall_hbm, wall, wall_sem)
    load_wall.start()

    barrier = pltpu.get_barrier_semaphore()
    for d in range(1, n_xsec):
        pl.semaphore_signal(
            barrier, inc=1, device_id=(v, lax.rem(h + d, n_xsec)), device_id_type=MESH
        )
    for sx in (1, -1):
        pl.semaphore_signal(barrier, inc=1, device_id=(v_side[sx], h), device_id_type=MESH)

    has_side = {1: h < n_xsec - 1, -1: h > 0}
    for sy in (1, -1):

        @pl.when(has_side[sy])
        def _(sy=sy):
            for sx in (1, -1):
                pl.semaphore_signal(
                    barrier, inc=1, device_id=(v_side[sx], h + sy), device_id_type=MESH
                )

        @pl.when(jnp.logical_not(has_side[sy]))
        def _(sy=sy):
            side = 0 if sy == -1 else 1
            for it in range(ITERS):
                ys_in[it, side] = jnp.zeros(ys_in.shape[2:], jnp.float32)
                for k, q in enumerate(CORNERS):
                    if LATTICE[q][1] == -sy:
                        cs_in[it, k] = jnp.zeros((8, LANES), jnp.float32)

    for copy in small_loads:
        copy.wait()

    row = lax.broadcasted_iota(jnp.int32, (8, LANES), 0)
    homes = [home[0, o] for o in range(owned)]
    places = []
    for o in range(owned):
        rank = jnp.int32(0)
        for p in range(o):
            rank = rank + (homes[p] == homes[o]).astype(jnp.int32)
        places.append(homes[o] * capacity + rank)
    for o in range(owned):
        blocks[o] = jnp.where(row == 6, 1.0, 0.0)
        for c in range(3):
            start = pos[c, o:o + 1, :]
            blocks[o, c:c + 1, :] = start
            blocks[o, 3 + c:4 + c, :] = start + shift[c, o:o + 1, :]
    values = [blocks[o] for o in range(owned)]
    for s in range(slots):
        total = None
        for o in range(owned):
            term = values[o] * (places[o] == s).astype(jnp.float32)
            total = term if total is None else total + term
        outgoing[s // capacity, s % capacity] = total

    sides = has_side[1].astype(jnp.int32) + has_side[-1].astype(jnp.int32)
    pl.semaphore_wait(barrier, n_xsec + 1 + 2 * sides)

    def exchange(source, target, send, recv):
        copies = []
        for d in range(1, n_xsec):
            peer = lax.rem(h + d, n_xsec)
            copy = pltpu.make_async_remote_copy(
                src_ref=source.at[peer],
                dst_ref=target.at[h],
                send_sem=send.at[d - 1],
                recv_sem=recv.at[d - 1],
                device_id=(v, peer),
                device_id_type=MESH,
            )
            copy.start()
            copies.append(copy)
        target[h] = source[h]
        return copies

    def moments_body(step, carry):
        rows = pl.ds(pl.multiple_of((step // tiles) * 16, 16), 16)
        lanes = pl.ds(pl.multiple_of((step % tiles) * LANES, LANES), LANES)
        density, momentum = moments([fbuf[q, rows, lanes] for q in range(Q)])
        mom[0, rows, lanes] = density
        for d in range(3):
            mom[1 + d, rows, lanes] = momentum[d]
        return carry

    def velocity_body(step, carry):
        rows = pl.ds(pl.multiple_of((step // tiles) * 16, 16), 16)
        lanes = pl.ds(pl.multiple_of((step % tiles) * LANES, LANES), LANES)
        density, momentum = moments([fbuf[q, rows, lanes] for q in range(Q)])
        mom[0, rows, lanes] = density
        inverse = 1.0 / density
        for d in range(3):
            mom[1 + d, rows, lanes] = momentum[d]
            value = (momentum[d] + 0.5 * force[d, rows, lanes]) * inverse
            vel[d, rows, lanes] = value
        return carry

    def collide_body(step, carry):
        rows = pl.ds(pl.multiple_of((step // tiles) * 8, 8), 8)
        lanes = pl.ds(pl.multiple_of((step % tiles) * LANES, LANES), LANES)
        density = mom[0, rows, lanes]
        inverse = 1.0 / density
        u = [
            (mom[1 + d, rows, lanes] + RELAX_TIME * force[d, rows, lanes]) * inverse
            for d in range(3)
        ]
        square = u[0] * u[0] + u[1] * u[1] + u[2] * u[2]
        solid = wall[rows, lanes] == 1
        gain = 1.0 / RELAX_TIME
        part = density * (1.0 - 1.5 * square)
        bases = {w: (gain * w) * part for w in sorted(set(WEIGHTS))}
        twice = {w: (2.0 * gain * w) * density for w in sorted(set(WEIGHTS))}
        half = [1.5 * component for component in u]
        f0 = fbuf[0, rows, lanes]
        rbuf[0, rows, lanes] = jnp.where(solid, f0, f0 * (1.0 - gain) + bases[WEIGHTS[0]])
        for q in range(1, Q, 2):
            o = OPPOSITE[q]
            along = signed_sum(
                [(LATTICE[q][d], half[d]) for d in range(3) if LATTICE[q][d] != 0]
            )
            fq = fbuf[q, rows, lanes]
            fo = fbuf[o, rows, lanes]
            odd = twice[WEIGHTS[q]] * along
            even = bases[WEIGHTS[q]] + odd * along
            rbuf[q, rows, lanes] = jnp.where(solid, fo, fq * (1.0 - gain) + (even + odd))
            rbuf[o, rows, lanes] = jnp.where(solid, fq, fo * (1.0 - gain) + (even - odd))
        return carry

    cell_x = lax.broadcasted_iota(jnp.int32, (extent_x, LANES), 0).astype(jnp.float32)
    cell_y = lax.broadcasted_iota(jnp.int32, (max(8, extent_y), LANES), 0).astype(jnp.float32)
    cell_z = lax.broadcasted_iota(jnp.int32, (NZ, LANES), 0).astype(jnp.float32)

    def hat(coordinate, cells):
        return jnp.maximum(0.0, 1.0 - jnp.abs(coordinate - cells))

    def weights_of(s):
        now = current[s]
        fixed = arrived[s // capacity, s % capacity]
        wx = hat(now[0:1], cell_x)
        wy = hat(now[1:2], cell_y)[:extent_y]
        wz = hat(now[2:3], cell_z)
        yz = jnp.concatenate([wy[j:j + 1] * wz for j in range(extent_y)], axis=0)
        pulls = [
            SPRING * (fixed[3 + c:4 + c] - now[c:c + 1]) * fixed[6:7] for c in range(3)
        ]
        lhs = jnp.concatenate([pull * wx for pull in pulls], axis=0)
        return wx, yz.astype(jnp.bfloat16), lhs.astype(jnp.bfloat16)

    copies = exchange(outgoing, arrived, a2a_send, a2a_recv)
    load.wait()
    load_wall.wait()
    lax.fori_loop(0, (extent_x // 16) * tiles, moments_body, 0, unroll=True)
    for copy in copies:
        copy.wait()
    for s in range(slots):
        current[s] = arrived[s // capacity, s % capacity]

    depth = lax.broadcasted_iota(jnp.int32, (extent_x, plane), 1) % NZ
    first_row = lax.broadcasted_iota(jnp.int32, (8, LANES), 0) == 0
    last_row = lax.broadcasted_iota(jnp.int32, (8, LANES), 0) == 7

    def shift_x(value, step_x, edge):
        width = value.shape[1]
        rolled = pltpu.roll(value, step_x % extent_x, 0)
        index = lax.broadcasted_iota(jnp.int32, (extent_x, width), 0)
        enters = index == (0 if step_x == 1 else extent_x - 1)
        return jnp.where(enters, jnp.broadcast_to(edge, (extent_x, width)), rolled)

    last_tile = pl.ds(plane - LANES, LANES)
    first_tile = pl.ds(0, LANES)

    for it in range(ITERS):
        parts = [weights_of(s) for s in range(slots)]
        left = jnp.concatenate([part[2] for part in parts], axis=1)
        wyz = jnp.concatenate([part[1] for part in parts], axis=1)
        field = lax.dot_general(
            left, wyz, (((1,), (1,)), ((), ())), preferred_element_type=jnp.float32
        )
        for d in range(3):
            force[d] = field[d * extent_x:(d + 1) * extent_x]
        lax.fori_loop(0, row_groups * tiles, collide_body, 0, unroll=4)

        sends = []
        for k, q in enumerate(CORNERS):
            sx, sy, _ = LATTICE[q]
            copy = pltpu.make_async_remote_copy(
                src_ref=rbuf.at[
                    q,
                    pl.ds(extent_x - 8 if sx == 1 else 0, 8),
                    last_tile if sy == 1 else first_tile,
                ],
                dst_ref=cs_in.at[it, k],
                send_sem=halo_send.at[it, 4 + k],
                recv_sem=halo_recv.at[it, 4 + k],
                device_id=(v_side[sx], h + sy),
                device_id_type=MESH,
            )
            sends.append((has_side[sy], has_side[-sy], copy))
        for can_send, _, copy in sends:

            @pl.when(can_send)
            def _(copy=copy):
                copy.start()

        for side, sx in enumerate((1, -1)):
            edge = extent_x - 1 if sx == 1 else 0
            for k, q in enumerate(X_DIRS[sx]):
                xs_out[it, side, k:k + 1, :] = rbuf[q, edge:edge + 1, :]
            copy = pltpu.make_async_remote_copy(
                src_ref=xs_out.at[it, side],
                dst_ref=xs_in.at[it, side],
                send_sem=halo_send.at[it, side],
                recv_sem=halo_recv.at[it, side],
                device_id=(v_side[sx], h),
                device_id_type=MESH,
            )
            copy.start()
            sends.append((None, None, copy))
        group = lax.broadcasted_iota(jnp.int32, (extent_x, LANES), 1) // NZ
        group8 = lax.broadcasted_iota(jnp.int32, (8, LANES), 1) // NZ
        for side, sy in enumerate((1, -1)):
            tile = last_tile if sy == 1 else first_tile
            origin = LANES - NZ if sy == 1 else 0
            dirs = Y_DIRS[sy]
            packed = None
            for g in range(GROUPS):
                part = pltpu.roll(rbuf[dirs[g], :, tile], (g * NZ - origin) % LANES, 1)
                packed = part if packed is None else jnp.where(group == g, part, packed)
            ys_out[it, side, 0:extent_x, :] = packed
            packed = None
            for g in range(row_groups):
                part = pltpu.roll(
                    rbuf[dirs[GROUPS], g * 8:(g + 1) * 8, tile], (g * NZ - origin) % LANES, 1
                )
                packed = part if packed is None else jnp.where(group8 == g, part, packed)
            ys_out[it, side, extent_x:extent_x + 8, :] = packed
            copy = pltpu.make_async_remote_copy(
                src_ref=ys_out.at[it, side],
                dst_ref=ys_in.at[it, side],
                send_sem=halo_send.at[it, 2 + side],
                recv_sem=halo_recv.at[it, 2 + side],
                device_id=(v, h + sy),
                device_id_type=MESH,
            )

            @pl.when(has_side[sy])
            def _(copy=copy):
                copy.start()

            sends.append((has_side[sy], has_side[-sy], copy))
        for q in range(Q):
            step_x, step_y, step_z = LATTICE[q]
            value = rbuf[q]
            if step_x != 0:
                value = pltpu.roll(value, step_x % extent_x, 0)
            amount = step_y * NZ + step_z
            if amount != 0:
                value = pltpu.roll(value, amount % plane, 1)
            if step_z != 0:
                value = jnp.where(depth == (0 if step_z == 1 else NZ - 1), 0.0, value)
            fbuf[q] = value

        for can_send, can_receive, copy in sends:
            if can_send is None:
                copy.wait_recv()
            else:

                @pl.when(can_receive)
                def _(copy=copy):
                    copy.wait_recv()

        for q in range(Q):
            step_x, step_y, step_z = LATTICE[q]
            amount = step_y * NZ + step_z
            if step_x != 0:
                side = 0 if step_x == 1 else 1
                edge = 0 if step_x == 1 else extent_x - 1
                k = X_DIRS[step_x].index(q)
                value = xs_in[it, side, k:k + 1, :]
                if amount != 0:
                    value = pltpu.roll(
                        jnp.broadcast_to(value, (8, plane)), amount % plane, 1
                    )[0:1]
                if step_z != 0:
                    value = jnp.where(depth[0:1] == (0 if step_z == 1 else NZ - 1), 0.0, value)
                fbuf[q, edge:edge + 1, :] = value
            if step_y != 0:
                side = 0 if step_y == 1 else 1
                origin = LANES - NZ if step_y == 1 else 0
                g = Y_DIRS[step_y].index(q)
                finish = origin + amount
                if g < GROUPS:
                    halo = pltpu.roll(
                        ys_in[it, side, 0:extent_x, :], (finish - g * NZ) % LANES, 1
                    )
                else:
                    folded = ys_in[it, side, extent_x:extent_x + 8, :]
                    halo = jnp.concatenate(
                        [
                            pltpu.roll(folded, (finish - r * NZ) % LANES, 1)
                            for r in range(row_groups)
                        ],
                        axis=0,
                    )
                if step_x != 0:
                    corner = pltpu.roll(cs_in[it, CORNERS.index(q)], amount % LANES, 1)
                    halo = shift_x(halo, step_x, corner[7:8] if step_x == 1 else corner[0:1])
                lane = lax.broadcasted_iota(jnp.int32, (extent_x, LANES), 1)
                if step_z != 0:
                    halo = jnp.where(lane % NZ == (0 if step_z == 1 else NZ - 1), 0.0, halo)
                tile = first_tile if step_y == 1 else last_tile
                enters = lane < NZ if step_y == 1 else lane >= LANES - NZ
                fbuf[q, :, tile] = jnp.where(enters, halo, fbuf[q, :, tile])
        for can_send, _, copy in sends:
            if can_send is None:
                copy.wait_send()
            else:

                @pl.when(can_send)
                def _(copy=copy):
                    copy.wait_send()

        lax.fori_loop(0, (extent_x // 16) * tiles, velocity_body, 0, unroll=True)
        flat = vel[...].reshape(3 * extent_x, plane).astype(jnp.bfloat16)
        sampled = jnp.dot(flat, wyz, preferred_element_type=jnp.float32)
        for s in range(slots):
            wx = hat(current[s, 0:1, :], cell_x)
            moves = [
                jnp.sum(
                    sampled[c * extent_x:(c + 1) * extent_x, s * LANES:(s + 1) * LANES] * wx,
                    axis=0,
                    keepdims=True,
                )
                for c in range(3)
            ]
            for c in range(3):
                current[s, c:c + 1, :] = current[s, c:c + 1, :] + moves[c]

    for s in range(slots):
        ret_out[s // capacity, s % capacity] = current[s] - arrived[s // capacity, s % capacity]
    back = exchange(ret_out, ret_in, ret_send, ret_recv)
    for copy in back:
        copy.wait()
    for o in range(owned):
        total = None
        for s in range(slots):
            term = ret_in[s // capacity, s % capacity] * (places[o] == s).astype(jnp.float32)
            total = term if total is None else total + term
        for c in range(3):
            disp[c, o:o + 1, :] = total[c:c + 1]


CHUNKS = 1


def hand_over(evolved_in, moved_in, evolved, moved, out_sem):
    size = -(-Q // CHUNKS)
    stores = [pltpu.make_async_copy(moved_in, moved, out_sem.at[CHUNKS])]
    for i, first in enumerate(range(0, Q, size)):
        part = pl.ds(first, min(size, Q - first))
        stores.append(
            pltpu.make_async_copy(evolved_in.at[part], evolved.at[part], out_sem.at[i])
        )
    for store in stores:
        store.start()
    for store in stores:
        store.wait()


def per_device(n_vessel, n_xsec, populations, wall_flags, positions, vertex_rest_shift, home_brick):
    owned = positions.shape[0]
    capacity = max(2, 2 * owned // n_xsec)
    slots = n_xsec * capacity
    extent_x, plane = populations.shape[1:]
    f32 = jnp.float32
    peers = max(1, n_xsec - 1)
    vmem = pl.BlockSpec(memory_space=pltpu.VMEM)
    hbm = pl.BlockSpec(memory_space=pltpu.HBM)
    exchange_shape = (n_xsec, capacity, 8, LANES)
    dma = pltpu.SemaphoreType.DMA
    evolved, moved = pl.pallas_call(
        functools.partial(kernel, n_vessel, n_xsec, capacity, extent_x, plane),
        out_shape=(
            pltpu.VMEM(populations.shape, f32),
            pltpu.VMEM((3, owned, LANES), f32),
        ),
        in_specs=[hbm] * 5,
        out_specs=(vmem, vmem),
        scratch_shapes=[
            pltpu.VMEM((extent_x, plane), jnp.int32),
            pltpu.VMEM((3, owned, LANES), f32),
            pltpu.VMEM((3, owned, LANES), f32),
            pltpu.SMEM((1, owned), jnp.int32),
            pltpu.VMEM((Q, extent_x, plane), f32),
            pltpu.VMEM((4, extent_x, plane), f32),
            pltpu.VMEM((3, extent_x, plane), f32),
            pltpu.VMEM((3, extent_x, plane), f32),
            pltpu.VMEM((owned, 8, LANES), f32),
            pltpu.VMEM(exchange_shape, f32),
            pltpu.VMEM(exchange_shape, f32),
            pltpu.VMEM((slots, 8, LANES), f32),
            pltpu.VMEM(exchange_shape, f32),
            pltpu.VMEM(exchange_shape, f32),
            pltpu.VMEM((ITERS, 2, len(X_DIRS[1]), plane), f32),
            pltpu.VMEM((ITERS, 2, len(X_DIRS[1]), plane), f32),
            pltpu.VMEM((ITERS, 2, extent_x + 8, LANES), f32),
            pltpu.VMEM((ITERS, 2, extent_x + 8, LANES), f32),
            pltpu.VMEM((ITERS, len(CORNERS), 8, LANES), f32),
            dma,
            dma,
            dma((3,)),
            dma((peers,)),
            dma((peers,)),
            dma((peers,)),
            dma((peers,)),
            dma((ITERS, 8)),
            dma((ITERS, 8)),
        ],
        compiler_params=pltpu.CompilerParams(
            collective_id=0, has_side_effects=True, vmem_limit_bytes=40 << 20
        ),
    )(
        *(
            pltpu.with_memory_space_constraint(value, pltpu.HBM)
            for value in (
                populations,
                wall_flags,
                jnp.transpose(positions, (1, 0, 2)),
                jnp.transpose(vertex_rest_shift, (1, 0, 2)),
                jnp.transpose(home_brick),
            )
        )
    )
    evolved, moved = pl.pallas_call(
        hand_over,
        out_shape=(
            jax.ShapeDtypeStruct(evolved.shape, f32),
            jax.ShapeDtypeStruct(moved.shape, f32),
        ),
        in_specs=[vmem, vmem],
        out_specs=(hbm, hbm),
        scratch_shapes=[dma((CHUNKS + 1,))],
        compiler_params=pltpu.CompilerParams(vmem_limit_bytes=1 << 20),
    )(
        pltpu.with_memory_space_constraint(evolved, pltpu.VMEM),
        pltpu.with_memory_space_constraint(moved, pltpu.VMEM),
    )
    return evolved, jnp.transpose(moved, (1, 0, 2))


def solution(mesh):
    in_specs = (
        P(None, "vessel", "xsec"),
        P("vessel", "xsec"),
        P(("vessel", "xsec"), None, None),
        P(("vessel", "xsec"), None, None),
        P(("vessel", "xsec"), None),
    )
    out_specs = (P(None, "vessel", "xsec"), P(("vessel", "xsec"), None, None))
    return jax.shard_map(
        functools.partial(per_device, mesh.shape["vessel"], mesh.shape["xsec"]),
        mesh=mesh,
        in_specs=in_specs,
        out_specs=out_specs,
        check_vma=False,
    )
```

```python
import functools

import jax
import jax.numpy as jnp
from jax import lax
from jax.experimental import pallas as pl
from jax.experimental.pallas import tpu as pltpu
from jax.sharding import PartitionSpec as P

NZ = 32
ITERS = 2
LATTICE = [
    [0, 0, 0],
    [1, 0, 0],
    [-1, 0, 0],
    [0, 1, 0],
    [0, -1, 0],
    [0, 0, 1],
    [0, 0, -1],
    [1, 1, 0],
    [-1, -1, 0],
    [1, -1, 0],
    [-1, 1, 0],
    [1, 0, 1],
    [-1, 0, -1],
    [1, 0, -1],
    [-1, 0, 1],
    [0, 1, 1],
    [0, -1, -1],
    [0, 1, -1],
    [0, -1, 1],
]
Q = len(LATTICE)
OPPOSITE = [0, 2, 1, 4, 3, 6, 5, 8, 7, 10, 9, 12, 11, 14, 13, 16, 15, 18, 17]
WEIGHTS = [1.0 / 3.0] + [1.0 / 18.0] * 6 + [1.0 / 36.0] * 12
RELAX_TIME = 0.8
SPRING = 0.1
LANES = 128
GROUPS = LANES // NZ
FAR = -8.0
MESH = pl.DeviceIdType.MESH
X_DIRS = {s: [q for q in range(Q) if LATTICE[q][0] == s] for s in (1, -1)}
Y_DIRS = {s: [q for q in range(Q) if LATTICE[q][1] == s] for s in (1, -1)}
CORNERS = [q for q in range(Q) if LATTICE[q][0] != 0 and LATTICE[q][1] != 0]


def signed_sum(terms):
    total = None
    for sign, value in terms:
        if total is None:
            total = value if sign > 0 else -value
        else:
            total = total + value if sign > 0 else total - value
    return total


def tree_sum(terms):
    while len(terms) > 1:
        terms = [
            terms[i] + terms[i + 1] if i + 1 < len(terms) else terms[i]
            for i in range(0, len(terms), 2)
        ]
    return terms[0]


def moments(fs):
    both = [fs[q] + fs[OPPOSITE[q]] for q in range(1, Q, 2)]
    flow = {q: fs[q] - fs[OPPOSITE[q]] for q in range(1, Q, 2)}
    density = tree_sum([fs[0]] + both)
    momentum = []
    for d in range(3):
        plus = tree_sum([flow[q] for q in flow if LATTICE[q][d] == 1])
        minus = [flow[q] for q in flow if LATTICE[q][d] == -1]
        momentum.append(plus - tree_sum(minus) if minus else plus)
    return density, momentum


def peers_by_distance(h, n):
    near = jnp.minimum(h, n - 1 - h)
    toward = jnp.where(h < n - 1 - h, 1, -1)
    order = [h]
    for k in range(1, n):
        step = (k + 1) // 2
        paired = h + step if k % 2 else h - step
        order.append(jnp.where(k <= 2 * near, paired, h + toward * (k - near)))
    return order


def kernel(
    n_vessel, n_xsec, capacity, extent_x, plane,
    pop_hbm, wall_hbm, pos_hbm, shift_hbm, home_hbm, fbuf, disp,
    wall, pos, shift, home, rbuf, mom, scale, force, vel,
    outgoing, arrived, current, ret_out, ret_in, wxs, left, wyz,
    xs_out, xs_in, ys_out, ys_in, cs_in,
    pop_sem, wall_sem, small_sem, a2a_send, a2a_recv, ret_send, ret_recv, halo_send, halo_recv,
):
    v = lax.axis_index("vessel")
    h = lax.axis_index("xsec")
    v_side = {1: lax.rem(v + 1, n_vessel), -1: lax.rem(v + n_vessel - 1, n_vessel)}
    owned = pos.shape[1]
    extent_y = plane // NZ
    tiles = plane // LANES
    row_groups = extent_x // 8
    order = peers_by_distance(h, n_xsec)
    has_side = {1: h < n_xsec - 1, -1: h > 0}

    barrier = pltpu.get_barrier_semaphore()
    for k in range(n_xsec - 1, 0, -1):
        pl.semaphore_signal(barrier, inc=1, device_id=(v, order[k]), device_id_type=MESH)
    for sx in (1, -1):
        pl.semaphore_signal(barrier, inc=1, device_id=(v_side[sx], h), device_id_type=MESH)
    small_loads = [
        pltpu.make_async_copy(source, target, small_sem.at[i])
        for i, (source, target) in enumerate(
            ((pos_hbm, pos), (shift_hbm, shift), (home_hbm, home))
        )
    ]
    for copy in small_loads:
        copy.start()
    load = pltpu.make_async_copy(pop_hbm, fbuf, pop_sem)
    load.start()
    load_wall = pltpu.make_async_copy(wall_hbm, wall, wall_sem)
    load_wall.start()

    for sy in (1, -1):

        @pl.when(has_side[sy])
        def _(sy=sy):
            for sx in (1, -1):
                pl.semaphore_signal(
                    barrier, inc=1, device_id=(v_side[sx], h + sy), device_id_type=MESH
                )

        @pl.when(jnp.logical_not(has_side[sy]))
        def _(sy=sy):
            side = 0 if sy == -1 else 1
            for it in range(ITERS):
                ys_in[it, side] = jnp.zeros(ys_in.shape[2:], jnp.float32)
                for k, q in enumerate(CORNERS):
                    if LATTICE[q][1] == -sy:
                        cs_in[it, k] = jnp.zeros((8, LANES), jnp.float32)

    for copy in small_loads:
        copy.wait()

    row = lax.broadcasted_iota(jnp.int32, (8, LANES), 0)
    upper = row < 4
    slot_row = row & 3
    homes = [home[0, o] for o in range(owned)]
    ranks = []
    for o in range(owned):
        rank = jnp.int32(0)
        for p in range(o):
            rank = rank + (homes[p] == homes[o]).astype(jnp.int32)
        ranks.append(rank)

    def spread_row(value, rows=8):
        return jnp.broadcast_to(value, (rows, LANES))

    sources = []
    for c in range(3):
        sources.append([])
        for o in range(owned):
            start = spread_row(pos[c, o:o + 1, :])
            rest = start + spread_row(shift[c, o:o + 1, :])
            sources[c].append(jnp.where(upper, start, rest))
    for p in range(n_xsec):
        chosen = [slot_row == jnp.where(homes[o] == p, ranks[o], 8) for o in range(owned)]
        for c in range(3):
            total = jnp.full((8, LANES), FAR, jnp.float32)
            for o in range(owned):
                total = jnp.where(chosen[o], sources[c][o], total)
            outgoing[p, c] = total
    place = jnp.full((8, LANES), -1, jnp.int32)
    for o in range(owned):
        place = jnp.where(row == o, homes[o] * capacity + ranks[o], place)

    sides = has_side[1].astype(jnp.int32) + has_side[-1].astype(jnp.int32)
    pl.semaphore_wait(barrier, n_xsec + 1 + 2 * sides)

    def transfer(source, target, send, recv, k):
        return pltpu.make_async_remote_copy(
            src_ref=source,
            dst_ref=target.at[h],
            send_sem=send.at[k],
            recv_sem=recv.at[h],
            device_id=(v, order[k]),
            device_id_type=MESH,
        )

    def arrival(target, send, recv, k):
        return pltpu.make_async_remote_copy(
            src_ref=target.at[order[k]],
            dst_ref=target.at[order[k]],
            send_sem=send.at[k],
            recv_sem=recv.at[order[k]],
            device_id=(v, order[k]),
            device_id_type=MESH,
        )

    outbound = [
        transfer(outgoing.at[order[k]], arrived, a2a_send, a2a_recv, k)
        for k in range(n_xsec - 1, 0, -1)
    ]
    for copy in outbound:
        copy.start()
    arrived[h] = outgoing[h]

    gain = 1.0 / RELAX_TIME

    def blocks_of(height):
        return [
            (pl.ds(r, height), pl.ds(t * LANES, LANES))
            for t in range(tiles)
            for r in range(0, extent_x, height)
        ]

    def prepare():
        for rows, lanes in blocks_of(8):
            fs = [fbuf[q, rows, lanes] for q in range(Q)]
            density, momentum = moments(fs)
            solid = wall[rows, lanes] == 1
            inverse = 1.0 / density
            mom[0, rows, lanes] = jnp.where(solid, 0.0, density)
            for d in range(3):
                mom[1 + d, rows, lanes] = momentum[d] * inverse
            scale[rows, lanes] = RELAX_TIME * inverse
            for q in range(Q):
                fbuf[q, rows, lanes] = jnp.where(solid, fs[OPPOSITE[q]], (1.0 - gain) * fs[q])

    def gather_moments():
        for rows, lanes in blocks_of(8):
            density, momentum = moments([fbuf[q, rows, lanes] for q in range(Q)])
            mom[0, rows, lanes] = density
            for d in range(3):
                mom[1 + d, rows, lanes] = momentum[d]

    def find_velocity(last):
        for rows, lanes in blocks_of(16):
            density = mom[0, rows, lanes]
            inverse = 1.0 / density
            half = 0.5 * inverse
            for d in range(3):
                moved = mom[1 + d, rows, lanes] * inverse
                value = moved + half * force[d, rows, lanes]
                vel[pl.ds(d * extent_x + rows.start, 16), lanes] = value.astype(jnp.bfloat16)
                if not last:
                    mom[1 + d, rows, lanes] = moved
            if not last:
                mom[0, rows, lanes] = jnp.where(wall[rows, lanes] == 1, 0.0, density)
                scale[rows, lanes] = RELAX_TIME * inverse

    def collide(rg, t, prepared):
        rows = pl.ds(rg * 8, 8)
        lanes = pl.ds(t * LANES, LANES)
        density = mom[0, rows, lanes]
        factor = scale[rows, lanes]
        u = [mom[1 + d, rows, lanes] + factor * force[d, rows, lanes] for d in range(3)]
        square = u[0] * u[0] + u[1] * u[1] + u[2] * u[2]
        part = density * (1.0 - 1.5 * square)
        bases = {w: (gain * w) * part for w in sorted(set(WEIGHTS))}
        twice = {w: (2.0 * gain * w) * density for w in sorted(set(WEIGHTS))}
        half = [1.5 * component for component in u]
        solid = None if prepared else wall[rows, lanes] == 1

        def write(q, own, other, change):
            if prepared:
                rbuf[q, rows, lanes] = own + change
            else:
                rbuf[q, rows, lanes] = jnp.where(solid, other, own * (1.0 - gain) + change)

        f0 = fbuf[0, rows, lanes]
        write(0, f0, f0, bases[WEIGHTS[0]])
        for q in range(1, Q, 2):
            o = OPPOSITE[q]
            along = signed_sum(
                [(LATTICE[q][d], half[d]) for d in range(3) if LATTICE[q][d] != 0]
            )
            fq = fbuf[q, rows, lanes]
            fo = fbuf[o, rows, lanes]
            odd = twice[WEIGHTS[q]] * along
            even = bases[WEIGHTS[q]] + odd * along
            write(q, fq, fo, even + odd)
            write(o, fo, fq, even - odd)

    cell_x = lax.broadcasted_iota(jnp.int32, (extent_x, LANES), 0).astype(jnp.float32)
    cell_y = lax.broadcasted_iota(jnp.int32, (max(8, extent_y), LANES), 0).astype(jnp.float32)
    cell_z = lax.broadcasted_iota(jnp.int32, (NZ, LANES), 0).astype(jnp.float32)

    def hat(coordinate, cells):
        return jnp.maximum(0.0, 1.0 - jnp.abs(coordinate - cells))

    width = capacity * LANES

    def group_lanes(k):
        return pl.ds(k * width, width)

    def build(it, k, now, fixed):
        pulls = [SPRING * (fixed[c] - now[c]) for c in range(3)]
        for j in range(capacity):
            lanes = pl.ds(k * width + j * LANES, LANES)
            wx = hat(now[0][j:j + 1], cell_x)
            wy = hat(now[1][j:j + 1], cell_y)
            wz = hat(now[2][j:j + 1], cell_z)
            wxs[it, k * capacity + j] = wx
            for y in range(extent_y):
                wyz[it, y * NZ:(y + 1) * NZ, lanes] = (wy[y:y + 1] * wz).astype(jnp.bfloat16)
            for c in range(3):
                left[it, c * extent_x:(c + 1) * extent_x, lanes] = (
                    pulls[c][j:j + 1] * wx
                ).astype(jnp.bfloat16)

    def spread(it, lanes):
        return lax.dot_general(
            left[it, :, lanes],
            wyz[it, :, lanes],
            (((1,), (1,)), ((), ())),
            preferred_element_type=jnp.float32,
        )

    def add_force(field, first):
        for d in range(3):
            part = field[d * extent_x:(d + 1) * extent_x]
            force[d] = part if first else force[d] + part

    def move(it, k):
        sampled = jnp.dot(
            vel[...], wyz[it, :, group_lanes(k)], preferred_element_type=jnp.float32
        )
        result = []
        for c in range(3):
            total = current[k, c]
            for j in range(capacity):
                part = sampled[c * extent_x:(c + 1) * extent_x, j * LANES:(j + 1) * LANES]
                step = jnp.sum(part * wxs[it, k * capacity + j], axis=0, keepdims=True)
                total = jnp.where(row == j, total + step, total)
            result.append(total)
        return result

    load.wait()
    load_wall.wait()
    prepare()
    for k in range(n_xsec):
        if k > 0:
            arrival(arrived, a2a_send, a2a_recv, k).wait_recv()
        now = [arrived[order[k], c] for c in range(3)]
        for c in range(3):
            current[k, c] = now[c]
        build(0, k, now, [pltpu.roll(now[c], 4, 0) for c in range(3)])
        add_force(spread(0, group_lanes(k)), k == 0)
    for copy in outbound:
        copy.wait_send()

    depth = lax.broadcasted_iota(jnp.int32, (extent_x, plane), 1) % NZ
    lane = lax.broadcasted_iota(jnp.int32, (extent_x, LANES), 1)
    line = lax.broadcasted_iota(jnp.int32, (1, plane), 1)

    def shift_x(value, step_x, edge):
        rolled = pltpu.roll(value, step_x % extent_x, 0)
        index = lax.broadcasted_iota(jnp.int32, value.shape, 0)
        enters = index == (0 if step_x == 1 else extent_x - 1)
        return jnp.where(enters, jnp.broadcast_to(edge, value.shape), rolled)

    last_tile = pl.ds(plane - LANES, LANES)
    first_tile = pl.ds(0, LANES)

    def halo_rows(it):
        for side, sx in enumerate((1, -1)):
            found = []
            for k, q in enumerate(X_DIRS[sx]):
                _, sy, sz = LATTICE[q]
                amount = sy * NZ + sz
                value = xs_in[it, side, k:k + 1, :]
                if amount != 0:
                    value = pltpu.roll(
                        jnp.broadcast_to(value, (8, plane)), amount % plane, 1
                    )[0:1]
                if sz != 0:
                    value = jnp.where(depth[0:1] == (0 if sz == 1 else NZ - 1), 0.0, value)
                if sy != 0:
                    outside = line < NZ if sy == 1 else line >= plane - NZ
                    value = jnp.where(outside, 0.0, value)
                found.append((q, value))
            yield (0 if sx == 1 else extent_x - 1), found

    def halo_tiles(it):
        for side, sy in enumerate((1, -1)):
            origin = LANES - NZ if sy == 1 else 0
            enters = lane < NZ if sy == 1 else lane >= LANES - NZ
            found = []
            for g, q in enumerate(Y_DIRS[sy]):
                sx, _, sz = LATTICE[q]
                amount = sy * NZ + sz
                finish = origin + amount
                if g < GROUPS:
                    value = pltpu.roll(
                        ys_in[it, side, 0:extent_x, :], (finish - g * NZ) % LANES, 1
                    )
                else:
                    folded = ys_in[it, side, extent_x:extent_x + 8, :]
                    value = jnp.concatenate(
                        [
                            pltpu.roll(folded, (finish - r * NZ) % LANES, 1)
                            for r in range(row_groups)
                        ],
                        axis=0,
                    )
                if sx != 0:
                    corner = pltpu.roll(cs_in[it, CORNERS.index(q)], amount % LANES, 1)
                    value = shift_x(value, sx, corner[7:8] if sx == 1 else corner[0:1])
                keep = enters
                if sz != 0:
                    keep = jnp.logical_and(enters, lane % NZ != (0 if sz == 1 else NZ - 1))
                found.append((q, jnp.where(keep, value, 0.0)))
            yield (first_tile if sy == 1 else last_tile), found

    def add_moments(found, where):
        mom[(0, *where)] = mom[(0, *where)] + tree_sum([value for _, value in found])
        for d in range(3):
            terms = [(LATTICE[q][d], value) for q, value in found if LATTICE[q][d] != 0]
            mom[(1 + d, *where)] = mom[(1 + d, *where)] + signed_sum(
                sorted(terms, key=lambda term: -term[0])
            )

    def halo_moments(it):
        for edge, found in halo_rows(it):
            add_moments(found, (slice(edge, edge + 1), slice(None)))
        for tile, found in halo_tiles(it):
            add_moments(found, (slice(None), tile))

    def halo_populations(it):
        for edge, found in halo_rows(it):
            for q, value in found:
                fbuf[q, edge:edge + 1, :] = value
        for tile, found in halo_tiles(it):
            for q, value in found:
                fbuf[q, :, tile] = fbuf[q, :, tile] + value

    group = lax.broadcasted_iota(jnp.int32, (extent_x, LANES), 1) // NZ
    group8 = lax.broadcasted_iota(jnp.int32, (8, LANES), 1) // NZ
    edge_groups = sorted({0, row_groups - 1})
    edge_tiles = sorted({0, tiles - 1})
    stages = [[], [], [], []]
    for rg in range(row_groups):
        for t in range(tiles):
            on_x, on_y = rg in edge_groups, t in edge_tiles
            stages[0 if on_x and on_y else 1 if on_x else 2 if on_y else 3].append((rg, t))

    def corner_copies(it):
        for k, q in enumerate(CORNERS):
            sx, sy, _ = LATTICE[q]
            copy = pltpu.make_async_remote_copy(
                src_ref=rbuf.at[
                    q,
                    pl.ds(extent_x - 8 if sx == 1 else 0, 8),
                    last_tile if sy == 1 else first_tile,
                ],
                dst_ref=cs_in.at[it, k],
                send_sem=halo_send.at[it, 4 + k],
                recv_sem=halo_recv.at[it, 4 + k],
                device_id=(v_side[sx], h + sy),
                device_id_type=MESH,
            )
            yield has_side[sy], has_side[-sy], copy

    def row_copies(it):
        for side, sx in enumerate((1, -1)):
            edge = extent_x - 1 if sx == 1 else 0
            for k, q in enumerate(X_DIRS[sx]):
                xs_out[it, side, k:k + 1, :] = rbuf[q, edge:edge + 1, :]
            yield None, None, pltpu.make_async_remote_copy(
                src_ref=xs_out.at[it, side],
                dst_ref=xs_in.at[it, side],
                send_sem=halo_send.at[it, side],
                recv_sem=halo_recv.at[it, side],
                device_id=(v_side[sx], h),
                device_id_type=MESH,
            )

    def tile_copies(it):
        for side, sy in enumerate((1, -1)):
            tile = last_tile if sy == 1 else first_tile
            origin = LANES - NZ if sy == 1 else 0
            dirs = Y_DIRS[sy]
            packed = None
            for g in range(GROUPS):
                part = pltpu.roll(rbuf[dirs[g], :, tile], (g * NZ - origin) % LANES, 1)
                packed = part if packed is None else jnp.where(group == g, part, packed)
            ys_out[it, side, 0:extent_x, :] = packed
            packed = None
            for g in range(row_groups):
                part = pltpu.roll(
                    rbuf[dirs[GROUPS], g * 8:(g + 1) * 8, tile], (g * NZ - origin) % LANES, 1
                )
                packed = part if packed is None else jnp.where(group8 == g, part, packed)
            ys_out[it, side, extent_x:extent_x + 8, :] = packed
            yield has_side[sy], has_side[-sy], pltpu.make_async_remote_copy(
                src_ref=ys_out.at[it, side],
                dst_ref=ys_in.at[it, side],
                send_sem=halo_send.at[it, 2 + side],
                recv_sem=halo_recv.at[it, 2 + side],
                device_id=(v, h + sy),
                device_id_type=MESH,
            )

    def guarded(condition, action):
        if condition is None:
            action()
        else:
            pl.when(condition)(action)

    def pass_on():
        for q in range(Q):
            step_x, step_y, step_z = LATTICE[q]
            value = rbuf[q]
            if step_x != 0:
                value = pltpu.roll(value, step_x % extent_x, 0)
            amount = step_y * NZ + step_z
            if amount != 0:
                value = pltpu.roll(value, amount % plane, 1)
            if step_z != 0:
                value = jnp.where(depth == (0 if step_z == 1 else NZ - 1), 0.0, value)
            if step_y != 0:
                column = lax.broadcasted_iota(jnp.int32, (extent_x, plane), 1)
                outside = column < NZ if step_y == 1 else column >= plane - NZ
                value = jnp.where(outside, 0.0, value)
            if step_x != 0:
                index = lax.broadcasted_iota(jnp.int32, (extent_x, plane), 0)
                value = jnp.where(index == (0 if step_x == 1 else extent_x - 1), 0.0, value)
            fbuf[q] = value

    pending = []
    for it in range(ITERS):
        last = it == ITERS - 1
        sends = []
        for stage, copies_of in zip(stages, (corner_copies, row_copies, tile_copies, None)):
            for rg, t in stage:
                collide(rg, t, it == 0)
            if copies_of is not None:
                for can_send, can_receive, copy in copies_of(it):
                    guarded(can_send, copy.start)
                    sends.append((can_send, can_receive, copy))
        pass_on()
        gather_moments()
        for _, can_receive, copy in sends:
            guarded(can_receive, copy.wait_recv)
        halo_moments(it)
        if not last:
            halo_populations(it)
        find_velocity(last)
        for can_send, _, copy in sends:
            guarded(can_send, copy.wait_send)
        if not last:
            for k in range(n_xsec):
                now = move(it, k)
                for c in range(3):
                    current[k, c] = now[c]
                build(it + 1, k, now, [pltpu.roll(arrived[order[k], c], 4, 0) for c in range(3)])
            add_force(spread(it + 1, slice(None)), True)

    for k in range(n_xsec - 1, -1, -1):
        now = move(ITERS - 1, k)
        moved = [now[c] - arrived[order[k], c] for c in range(3)]
        ret_out[k, 0] = jnp.where(upper, moved[0], pltpu.roll(moved[1], 4, 0))
        ret_out[k, 1] = moved[2]
        if k > 0:
            copy = transfer(ret_out.at[k], ret_in, ret_send, ret_recv, k)
            copy.start()
            pending.append(copy)
    halo_populations(ITERS - 1)
    totals = [jnp.zeros((8, LANES), jnp.float32) for _ in range(3)]
    for k in range(n_xsec):
        if k > 0:
            arrival(ret_in, ret_send, ret_recv, k).wait_recv()
        found = [ret_out[0, i] if k == 0 else ret_in[order[k], i] for i in range(2)]
        for j in range(capacity):
            here = place == order[k] * capacity + j
            for c in range(3):
                line_index = (c * 4 + j) % 8
                value = found[c // 2][line_index:line_index + 1]
                totals[c] = jnp.where(here, spread_row(value), totals[c])
    for c in range(3):
        disp[c] = totals[c][0:owned]
    for copy in pending:
        copy.wait_send()


CHUNKS = 1


def hand_over(evolved_in, moved_in, evolved, moved, out_sem):
    size = -(-Q // CHUNKS)
    stores = [pltpu.make_async_copy(moved_in, moved, out_sem.at[CHUNKS])]
    for i, first in enumerate(range(0, Q, size)):
        part = pl.ds(first, min(size, Q - first))
        stores.append(
            pltpu.make_async_copy(evolved_in.at[part], evolved.at[part], out_sem.at[i])
        )
    for store in stores:
        store.start()
    for store in stores:
        store.wait()


def per_device(n_vessel, n_xsec, populations, wall_flags, positions, vertex_rest_shift, home_brick):
    owned = positions.shape[0]
    capacity = max(2, 2 * owned // n_xsec)
    slots = n_xsec * capacity
    extent_x, plane = populations.shape[1:]
    f32 = jnp.float32
    vmem = pl.BlockSpec(memory_space=pltpu.VMEM)
    hbm = pl.BlockSpec(memory_space=pltpu.HBM)
    dma = pltpu.SemaphoreType.DMA
    evolved, moved = pl.pallas_call(
        functools.partial(kernel, n_vessel, n_xsec, capacity, extent_x, plane),
        out_shape=(
            pltpu.VMEM(populations.shape, f32),
            pltpu.VMEM((3, owned, LANES), f32),
        ),
        in_specs=[hbm] * 5,
        out_specs=(vmem, vmem),
        scratch_shapes=[
            pltpu.VMEM((extent_x, plane), jnp.int32),
            pltpu.VMEM((3, owned, LANES), f32),
            pltpu.VMEM((3, owned, LANES), f32),
            pltpu.SMEM((1, owned), jnp.int32),
            pltpu.VMEM((Q, extent_x, plane), f32),
            pltpu.VMEM((4, extent_x, plane), f32),
            pltpu.VMEM((extent_x, plane), f32),
            pltpu.VMEM((3, extent_x, plane), f32),
            pltpu.VMEM((3 * extent_x, plane), jnp.bfloat16),
            pltpu.VMEM((n_xsec, 3, 8, LANES), f32),
            pltpu.VMEM((n_xsec, 3, 8, LANES), f32),
            pltpu.VMEM((n_xsec, 3, 8, LANES), f32),
            pltpu.VMEM((n_xsec, 2, 8, LANES), f32),
            pltpu.VMEM((n_xsec, 2, 8, LANES), f32),
            pltpu.VMEM((ITERS, slots, extent_x, LANES), f32),
            pltpu.VMEM((ITERS, 3 * extent_x, slots * LANES), jnp.bfloat16),
            pltpu.VMEM((ITERS, plane, slots * LANES), jnp.bfloat16),
            pltpu.VMEM((ITERS, 2, len(X_DIRS[1]), plane), f32),
            pltpu.VMEM((ITERS, 2, len(X_DIRS[1]), plane), f32),
            pltpu.VMEM((ITERS, 2, extent_x + 8, LANES), f32),
            pltpu.VMEM((ITERS, 2, extent_x + 8, LANES), f32),
            pltpu.VMEM((ITERS, len(CORNERS), 8, LANES), f32),
            dma,
            dma,
            dma((3,)),
            dma((n_xsec,)),
            dma((n_xsec,)),
            dma((n_xsec,)),
            dma((n_xsec,)),
            dma((ITERS, 8)),
            dma((ITERS, 8)),
        ],
        compiler_params=pltpu.CompilerParams(
            collective_id=0, has_side_effects=True, vmem_limit_bytes=40 << 20
        ),
    )(
        *(
            pltpu.with_memory_space_constraint(value, pltpu.HBM)
            for value in (
                populations,
                wall_flags,
                jnp.transpose(positions, (1, 0, 2)),
                jnp.transpose(vertex_rest_shift, (1, 0, 2)),
                jnp.transpose(home_brick),
            )
        )
    )
    evolved, moved = pl.pallas_call(
        hand_over,
        out_shape=(
            jax.ShapeDtypeStruct(evolved.shape, f32),
            jax.ShapeDtypeStruct(moved.shape, f32),
        ),
        in_specs=[vmem, vmem],
        out_specs=(hbm, hbm),
        scratch_shapes=[dma((CHUNKS + 1,))],
        compiler_params=pltpu.CompilerParams(vmem_limit_bytes=1 << 20),
    )(
        pltpu.with_memory_space_constraint(evolved, pltpu.VMEM),
        pltpu.with_memory_space_constraint(moved, pltpu.VMEM),
    )
    return evolved, jnp.transpose(moved, (1, 0, 2))


def solution(mesh):
    in_specs = (
        P(None, "vessel", "xsec"),
        P("vessel", "xsec"),
        P(("vessel", "xsec"), None, None),
        P(("vessel", "xsec"), None, None),
        P(("vessel", "xsec"), None),
    )
    out_specs = (P(None, "vessel", "xsec"), P(("vessel", "xsec"), None, None))
    return jax.shard_map(
        functools.partial(per_device, mesh.shape["vessel"], mesh.shape["xsec"]),
        mesh=mesh,
        in_specs=in_specs,
        out_specs=out_specs,
        check_vma=False,
    )
```

```python
import functools

import jax
import jax.numpy as jnp
from jax import lax
from jax.experimental import pallas as pl
from jax.experimental.pallas import tpu as pltpu
from jax.sharding import PartitionSpec as P

NZ = 32
ITERS = 2
LATTICE = [
    [0, 0, 0],
    [1, 0, 0],
    [-1, 0, 0],
    [0, 1, 0],
    [0, -1, 0],
    [0, 0, 1],
    [0, 0, -1],
    [1, 1, 0],
    [-1, -1, 0],
    [1, -1, 0],
    [-1, 1, 0],
    [1, 0, 1],
    [-1, 0, -1],
    [1, 0, -1],
    [-1, 0, 1],
    [0, 1, 1],
    [0, -1, -1],
    [0, 1, -1],
    [0, -1, 1],
]
Q = len(LATTICE)
OPPOSITE = [0, 2, 1, 4, 3, 6, 5, 8, 7, 10, 9, 12, 11, 14, 13, 16, 15, 18, 17]
WEIGHTS = [1.0 / 3.0] + [1.0 / 18.0] * 6 + [1.0 / 36.0] * 12
RELAX_TIME = 0.8
SPRING = 0.1
LANES = 128
GROUPS = LANES // NZ
FAR = -8.0
MESH = pl.DeviceIdType.MESH
X_DIRS = {s: [q for q in range(Q) if LATTICE[q][0] == s] for s in (1, -1)}
Y_DIRS = {s: [q for q in range(Q) if LATTICE[q][1] == s] for s in (1, -1)}
CORNERS = [q for q in range(Q) if LATTICE[q][0] != 0 and LATTICE[q][1] != 0]


def signed_sum(terms):
    total = None
    for sign, value in terms:
        if total is None:
            total = value if sign > 0 else -value
        else:
            total = total + value if sign > 0 else total - value
    return total


def tree_sum(terms):
    while len(terms) > 1:
        terms = [
            terms[i] + terms[i + 1] if i + 1 < len(terms) else terms[i]
            for i in range(0, len(terms), 2)
        ]
    return terms[0]


def moments(fs):
    both = [fs[q] + fs[OPPOSITE[q]] for q in range(1, Q, 2)]
    flow = {q: fs[q] - fs[OPPOSITE[q]] for q in range(1, Q, 2)}
    density = tree_sum([fs[0]] + both)
    momentum = []
    for d in range(3):
        plus = tree_sum([flow[q] for q in flow if LATTICE[q][d] == 1])
        minus = [flow[q] for q in flow if LATTICE[q][d] == -1]
        momentum.append(plus - tree_sum(minus) if minus else plus)
    return density, momentum


def peers_by_distance(h, n):
    near = jnp.minimum(h, n - 1 - h)
    toward = jnp.where(h < n - 1 - h, 1, -1)
    order = [h]
    for k in range(1, n):
        step = (k + 1) // 2
        paired = h + step if k % 2 else h - step
        order.append(jnp.where(k <= 2 * near, paired, h + toward * (k - near)))
    return order


def kernel(
    n_vessel, n_xsec, capacity, extent_x, plane,
    pop_hbm, wall_hbm, pos_hbm, shift_hbm, home_hbm, fbuf, disp,
    wall, points, home, rbuf, mom, scale, force, vel,
    outgoing, arrived, current, ret_out, ret_in, wxs,
    xs_out, xs_in, ys_out, ys_in, cs_in,
    load_sem, out_sem, a2a_recv, ret_recv, halo_send, halo_recv,
):
    v = lax.axis_index("vessel")
    h = lax.axis_index("xsec")
    v_side = {1: lax.rem(v + 1, n_vessel), -1: lax.rem(v + n_vessel - 1, n_vessel)}
    owned = points.shape[2]
    pos, shift = points.at[0], points.at[1]
    extent_y = plane // NZ
    tiles = plane // LANES
    row_groups = extent_x // 8
    order = peers_by_distance(h, n_xsec)
    has_side = {1: h < n_xsec - 1, -1: h > 0}

    barrier = pltpu.get_barrier_semaphore()
    for k in range(n_xsec - 1, 0, -1):
        pl.semaphore_signal(barrier, inc=1, device_id=(v, order[k]), device_id_type=MESH)
    for sx in (1, -1):
        pl.semaphore_signal(barrier, inc=1, device_id=(v_side[sx], h), device_id_type=MESH)
    small_loads = [
        pltpu.make_async_copy(source, target, load_sem.at[i])
        for i, source, target in ((0, pos_hbm, pos), (0, shift_hbm, shift), (1, home_hbm, home))
    ]
    for copy in small_loads:
        copy.start()
    load = pltpu.make_async_copy(pop_hbm, fbuf, load_sem.at[2])
    load.start()
    load_wall = pltpu.make_async_copy(wall_hbm, wall, load_sem.at[3])
    load_wall.start()

    for sy in (1, -1):

        @pl.when(has_side[sy])
        def _(sy=sy):
            for sx in (1, -1):
                pl.semaphore_signal(
                    barrier, inc=1, device_id=(v_side[sx], h + sy), device_id_type=MESH
                )

        @pl.when(jnp.logical_not(has_side[sy]))
        def _(sy=sy):
            side = 0 if sy == -1 else 1
            for it in range(ITERS):
                ys_in[it, side] = jnp.zeros(ys_in.shape[2:], jnp.float32)
                for k, q in enumerate(CORNERS):
                    if LATTICE[q][1] == -sy:
                        cs_in[it, k] = jnp.zeros((8, LANES), jnp.float32)

    pltpu.make_async_copy(points, points, load_sem.at[0]).wait()
    small_loads[2].wait()

    row = lax.broadcasted_iota(jnp.int32, (8, LANES), 0)
    odd_row = (row & 1) == 1
    slot_row = row >> 1
    homes = [home[0, o] for o in range(owned)]
    ranks = []
    for o in range(owned):
        rank = jnp.int32(0)
        for p in range(o):
            rank = rank + (homes[p] == homes[o]).astype(jnp.int32)
        ranks.append(rank)

    def spread_row(value, rows=8):
        return jnp.broadcast_to(value, (rows, LANES))

    sources = []
    for c in range(3):
        sources.append([])
        for o in range(owned):
            start = spread_row(pos[c, o:o + 1, :])
            rest = start + spread_row(shift[c, o:o + 1, :])
            sources[c].append(jnp.where(odd_row, start, rest))
    for p in range(n_xsec):
        chosen = [slot_row == jnp.where(homes[o] == p, ranks[o], 8) for o in range(owned)]
        for c in range(3):
            total = jnp.full((8, LANES), FAR, jnp.float32)
            for o in range(owned):
                total = jnp.where(chosen[o], sources[c][o], total)
            outgoing[p, c] = total
    place = jnp.full((8, LANES), -1, jnp.int32)
    for o in range(owned):
        place = jnp.where(row == o, homes[o] * capacity + ranks[o], place)

    sides = has_side[1].astype(jnp.int32) + has_side[-1].astype(jnp.int32)
    pl.semaphore_wait(barrier, n_xsec + 1 + 2 * sides)

    def slot_of(sender, receiver):
        return lax.rem(sender - receiver + n_xsec - 1, n_xsec)

    def transfer(source, target, send, recv, k):
        return pltpu.make_async_remote_copy(
            src_ref=source,
            dst_ref=target.at[h],
            send_sem=send,
            recv_sem=recv.at[slot_of(h, order[k])],
            device_id=(v, order[k]),
            device_id_type=MESH,
        )

    def arrival(target, send, recv, k):
        return pltpu.make_async_remote_copy(
            src_ref=target.at[order[k]],
            dst_ref=target.at[order[k]],
            send_sem=send,
            recv_sem=recv.at[slot_of(order[k], h)],
            device_id=(v, order[k]),
            device_id_type=MESH,
        )

    outbound = [
        transfer(outgoing.at[order[k]], arrived, out_sem.at[0], a2a_recv, k)
        for k in range(n_xsec - 1, 0, -1)
    ]
    for copy in outbound:
        copy.start()
    arrived[h] = outgoing[h]

    gain = 1.0 / RELAX_TIME

    def blocks_of(height):
        return [
            (pl.ds(r, height), pl.ds(t * LANES, LANES))
            for t in range(tiles)
            for r in range(0, extent_x, height)
        ]

    def prepare():
        for rows, lanes in blocks_of(8):
            fs = [fbuf[q, rows, lanes] for q in range(Q)]
            density, momentum = moments(fs)
            solid = wall[rows, lanes] == 1
            inverse = 1.0 / density
            mom[0, rows, lanes] = jnp.where(solid, 0.0, density)
            for d in range(3):
                mom[1 + d, rows, lanes] = momentum[d] * inverse
            scale[rows, lanes] = RELAX_TIME * inverse
            for q in range(Q):
                fbuf[q, rows, lanes] = jnp.where(solid, fs[OPPOSITE[q]], (1.0 - gain) * fs[q])

    def gather_moments():
        for rows, lanes in blocks_of(8):
            density, momentum = moments([fbuf[q, rows, lanes] for q in range(Q)])
            mom[0, rows, lanes] = density
            for d in range(3):
                mom[1 + d, rows, lanes] = momentum[d]

    def find_velocity(last):
        for rows, lanes in blocks_of(16):
            density = mom[0, rows, lanes]
            inverse = 1.0 / density
            half = 0.5 * inverse
            for d in range(3):
                moved = mom[1 + d, rows, lanes] * inverse
                value = moved + half * force[d, rows, lanes]
                vel[lanes.start // LANES, pl.ds(d * extent_x + rows.start, 16)] = value.astype(
                    jnp.bfloat16
                )
                if not last:
                    mom[1 + d, rows, lanes] = moved
            if not last:
                mom[0, rows, lanes] = jnp.where(wall[rows, lanes] == 1, 0.0, density)
                scale[rows, lanes] = RELAX_TIME * inverse

    def collide(rg, t, prepared):
        rows = pl.ds(rg * 8, 8)
        lanes = pl.ds(t * LANES, LANES)
        density = mom[0, rows, lanes]
        factor = scale[rows, lanes]
        u = [mom[1 + d, rows, lanes] + factor * force[d, rows, lanes] for d in range(3)]
        square = u[0] * u[0] + u[1] * u[1] + u[2] * u[2]
        part = density * (1.0 - 1.5 * square)
        bases = {w: (gain * w) * part for w in sorted(set(WEIGHTS))}
        twice = {w: (2.0 * gain * w) * density for w in sorted(set(WEIGHTS))}
        half = [1.5 * component for component in u]

        solid = None if prepared else wall[rows, lanes] == 1

        def write(q, own, other, change):
            if prepared:
                rbuf[q, rows, lanes] = own + change
            else:
                rbuf[q, rows, lanes] = jnp.where(solid, other, own * (1.0 - gain) + change)

        f0 = fbuf[0, rows, lanes]
        write(0, f0, f0, bases[WEIGHTS[0]])
        for q in range(1, Q, 2):
            o = OPPOSITE[q]
            along = signed_sum(
                [(LATTICE[q][d], half[d]) for d in range(3) if LATTICE[q][d] != 0]
            )
            fq = fbuf[q, rows, lanes]
            fo = fbuf[o, rows, lanes]
            odd = twice[WEIGHTS[q]] * along
            even = bases[WEIGHTS[q]] + odd * along
            write(q, fq, fo, even + odd)
            write(o, fo, fq, even - odd)

    cell_x = lax.broadcasted_iota(jnp.int32, (extent_x, LANES), 0).astype(jnp.float32)
    cell_y = lax.broadcasted_iota(jnp.int32, (max(8, extent_y), LANES), 0).astype(jnp.float32)
    cell_z = lax.broadcasted_iota(jnp.int32, (NZ, LANES), 0).astype(jnp.float32)

    def hat(coordinate, cells):
        return jnp.maximum(0.0, 1.0 - jnp.abs(coordinate - cells))

    def build(it, k, now, fixed):
        pulls = [SPRING * (fixed[c] - now[c]) for c in range(3)]
        sides, planes = [], []
        for j in range(capacity):
            at = slice(2 * j + 1, 2 * j + 2)
            wx = hat(now[0][at], cell_x)
            wy = hat(now[1][at], cell_y)
            wz = hat(now[2][at], cell_z)
            wxs[it, k * capacity + j] = wx
            flat = jnp.concatenate([wy[y:y + 1] * wz for y in range(extent_y)], axis=0)
            planes.append(flat.astype(jnp.bfloat16))
            side = jnp.concatenate([pulls[c][at] * wx for c in range(3)], axis=0)
            sides.append(side.astype(jnp.bfloat16))
        return jnp.concatenate(sides, axis=1), jnp.concatenate(planes, axis=1)

    def spread(sides, planes):
        return lax.dot_general(
            sides, planes, (((1,), (1,)), ((), ())), preferred_element_type=jnp.float32
        )

    def spread_t(sides, planes):
        field = lax.dot_general(
            planes, sides, (((1,), (1,)), ((), ())), preferred_element_type=jnp.float32
        )
        field = jnp.concatenate([field, jnp.zeros((plane, LANES - 3 * extent_x), jnp.float32)], axis=1)
        return jnp.transpose(field)[0:3 * extent_x]

    def add_force(field, first):
        for d in range(3):
            part = field[d * extent_x:(d + 1) * extent_x]
            force[d] = part if first else force[d] + part

    low_rows = row < 4
    mid_rows = jnp.logical_and(row >= 2, row < 6)
    second = (row & 2) != 0

    def merge(mask, a, b, shift):
        return jnp.where(mask, a, b) + pltpu.roll(jnp.where(mask, b, a), shift, 0)

    def row_sums(parts):
        parts = parts + [jnp.zeros((8, LANES), jnp.float32)] * (4 - len(parts))
        pairs = merge(low_rows, parts[1], parts[3], 4), merge(mid_rows, parts[2], parts[0], 4)
        total = merge(second, pairs[0], pairs[1], 2)
        return total + pltpu.roll(total, 1, 0)

    def move(it, k, planes):
        flow = jnp.concatenate([vel[t] for t in range(tiles)], axis=1)
        sampled = jnp.dot(flow, planes, preferred_element_type=jnp.float32)
        result = []
        for c in range(3):
            parts = []
            for j in range(capacity):
                part = sampled[c * extent_x:(c + 1) * extent_x, j * LANES:(j + 1) * LANES]
                part = part * wxs[it, k * capacity + j]
                parts.append(tree_sum([part[i:i + 8] for i in range(0, extent_x, 8)]))
            result.append(current[k, c] + row_sums(parts))
        return result

    load.wait()
    load_wall.wait()
    prepare()
    planes = []
    for k in range(n_xsec):
        if k > 0:
            arrival(arrived, out_sem.at[0], a2a_recv, k).wait_recv()
        now = [arrived[order[k], c] for c in range(3)]
        for c in range(3):
            current[k, c] = now[c]
        sides, flat = build(0, k, now, [pltpu.roll(now[c], 1, 0) for c in range(3)])
        planes.append(flat)
        add_force(spread(sides, flat), k == 0)

    depth = lax.broadcasted_iota(jnp.int32, (extent_x, plane), 1) % NZ
    lane = lax.broadcasted_iota(jnp.int32, (extent_x, LANES), 1)
    line = lax.broadcasted_iota(jnp.int32, (1, plane), 1)

    def shift_x(value, step_x, edge):
        rolled = pltpu.roll(value, step_x % extent_x, 0)
        index = lax.broadcasted_iota(jnp.int32, value.shape, 0)
        enters = index == (0 if step_x == 1 else extent_x - 1)
        return jnp.where(enters, jnp.broadcast_to(edge, value.shape), rolled)

    last_tile = pl.ds(plane - LANES, LANES)
    first_tile = pl.ds(0, LANES)

    def halo_rows(it):
        for side, sx in enumerate((1, -1)):
            found = []
            for k, q in enumerate(X_DIRS[sx]):
                _, sy, sz = LATTICE[q]
                amount = sy * NZ + sz
                value = xs_in[it, side, k:k + 1, :]
                if amount != 0:
                    value = pltpu.roll(
                        jnp.broadcast_to(value, (8, plane)), amount % plane, 1
                    )[0:1]
                if sz != 0:
                    value = jnp.where(depth[0:1] == (0 if sz == 1 else NZ - 1), 0.0, value)
                if sy != 0:
                    outside = line < NZ if sy == 1 else line >= plane - NZ
                    value = jnp.where(outside, 0.0, value)
                found.append((q, value))
            yield (0 if sx == 1 else extent_x - 1), found

    def halo_tiles(it):
        for side, sy in enumerate((1, -1)):
            origin = LANES - NZ if sy == 1 else 0
            enters = lane < NZ if sy == 1 else lane >= LANES - NZ
            found = []
            for g, q in enumerate(Y_DIRS[sy]):
                sx, _, sz = LATTICE[q]
                amount = sy * NZ + sz
                finish = origin + amount
                if g < GROUPS:
                    value = pltpu.roll(
                        ys_in[it, side, 0:extent_x, :], (finish - g * NZ) % LANES, 1
                    )
                else:
                    folded = ys_in[it, side, extent_x:extent_x + 8, :]
                    value = jnp.concatenate(
                        [
                            pltpu.roll(folded, (finish - r * NZ) % LANES, 1)
                            for r in range(row_groups)
                        ],
                        axis=0,
                    )
                if sx != 0:
                    corner = pltpu.roll(cs_in[it, CORNERS.index(q)], amount % LANES, 1)
                    value = shift_x(value, sx, corner[7:8] if sx == 1 else corner[0:1])
                keep = enters
                if sz != 0:
                    keep = jnp.logical_and(enters, lane % NZ != (0 if sz == 1 else NZ - 1))
                found.append((q, jnp.where(keep, value, 0.0)))
            yield (first_tile if sy == 1 else last_tile), found

    def add_moments(found, where):
        mom[(0, *where)] = mom[(0, *where)] + tree_sum([value for _, value in found])
        for d in range(3):
            terms = [(LATTICE[q][d], value) for q, value in found if LATTICE[q][d] != 0]
            mom[(1 + d, *where)] = mom[(1 + d, *where)] + signed_sum(
                sorted(terms, key=lambda term: -term[0])
            )

    def halo_values(it):
        return list(halo_rows(it)), list(halo_tiles(it))

    def halo_moments(values):
        for edge, found in values[0]:
            add_moments(found, (slice(edge, edge + 1), slice(None)))
        for tile, found in values[1]:
            add_moments(found, (slice(None), tile))

    def halo_populations(values):
        for edge, found in values[0]:
            for q, value in found:
                fbuf[q, edge:edge + 1, :] = value
        for tile, found in values[1]:
            for q, value in found:
                fbuf[q, :, tile] = fbuf[q, :, tile] + value

    group = lax.broadcasted_iota(jnp.int32, (extent_x, LANES), 1) // NZ
    group8 = lax.broadcasted_iota(jnp.int32, (8, LANES), 1) // NZ
    edge_groups = sorted({0, row_groups - 1})
    side_tiles = {1: tiles - 1, -1: 0}
    stages = {1: [], -1: [], 0: [], None: []}
    for rg in range(row_groups):
        for t in range(tiles):
            if t == side_tiles[1]:
                stages[1].append((rg, t))
            elif t == side_tiles[-1]:
                stages[-1].append((rg, t))
            elif rg in edge_groups:
                stages[0].append((rg, t))
            else:
                stages[None].append((rg, t))

    def corner_copies(it, side):
        for k, q in enumerate(CORNERS):
            sx, sy, _ = LATTICE[q]
            if sy != side:
                continue
            copy = pltpu.make_async_remote_copy(
                src_ref=rbuf.at[
                    q,
                    pl.ds(extent_x - 8 if sx == 1 else 0, 8),
                    last_tile if sy == 1 else first_tile,
                ],
                dst_ref=cs_in.at[it, k],
                send_sem=halo_send.at[it, 2],
                recv_sem=halo_recv.at[it, 2],
                device_id=(v_side[sx], h + sy),
                device_id_type=MESH,
            )
            yield has_side[sy], copy

    def row_copies(it):
        for side, sx in enumerate((1, -1)):
            edge = extent_x - 1 if sx == 1 else 0
            for k, q in enumerate(X_DIRS[sx]):
                xs_out[it, side, k:k + 1, :] = rbuf[q, edge:edge + 1, :]
            yield None, pltpu.make_async_remote_copy(
                src_ref=xs_out.at[it, side],
                dst_ref=xs_in.at[it, side],
                send_sem=halo_send.at[it, 0],
                recv_sem=halo_recv.at[it, 0],
                device_id=(v_side[sx], h),
                device_id_type=MESH,
            )

    def tile_copies(it, sy):
        for side in (0,) if sy == 1 else (1,):
            tile = last_tile if sy == 1 else first_tile
            origin = LANES - NZ if sy == 1 else 0
            dirs = Y_DIRS[sy]
            packed = None
            for g in range(GROUPS):
                part = pltpu.roll(rbuf[dirs[g], :, tile], (g * NZ - origin) % LANES, 1)
                packed = part if packed is None else jnp.where(group == g, part, packed)
            ys_out[it, side, 0:extent_x, :] = packed
            packed = None
            for g in range(row_groups):
                part = pltpu.roll(
                    rbuf[dirs[GROUPS], g * 8:(g + 1) * 8, tile], (g * NZ - origin) % LANES, 1
                )
                packed = part if packed is None else jnp.where(group8 == g, part, packed)
            ys_out[it, side, extent_x:extent_x + 8, :] = packed
            yield has_side[sy], pltpu.make_async_remote_copy(
                src_ref=ys_out.at[it, side],
                dst_ref=ys_in.at[it, side],
                send_sem=halo_send.at[it, 1],
                recv_sem=halo_recv.at[it, 1],
                device_id=(v, h + sy),
                device_id_type=MESH,
            )

    def settle(it, sent):
        def wait(kind, ref):
            copy = pltpu.make_async_remote_copy(
                src_ref=ref,
                dst_ref=ref,
                send_sem=halo_send.at[it, kind],
                recv_sem=halo_recv.at[it, kind],
                device_id=(v_side[1], h),
                device_id_type=MESH,
            )
            return copy.wait_send if sent else copy.wait_recv

        between = jnp.logical_and(has_side[1], has_side[-1])
        half = len(CORNERS) // 2
        pl.when(between)(wait(2, cs_in.at[it]))
        pl.when(jnp.logical_not(between))(wait(2, cs_in.at[it, pl.ds(0, half)]))
        pl.when(between)(wait(1, ys_in.at[it]))
        pl.when(jnp.logical_not(between))(wait(1, ys_in.at[it, pl.ds(0, 1)]))
        wait(0, xs_in.at[it])()

    def pass_on():
        for q in range(Q):
            step_x, step_y, step_z = LATTICE[q]
            value = rbuf[q]
            if step_x != 0:
                value = pltpu.roll(value, step_x % extent_x, 0)
            amount = step_y * NZ + step_z
            if amount != 0:
                value = pltpu.roll(value, amount % plane, 1)
            if step_z != 0:
                value = jnp.where(depth == (0 if step_z == 1 else NZ - 1), 0.0, value)
            if step_y != 0:
                column = lax.broadcasted_iota(jnp.int32, (extent_x, plane), 1)
                outside = column < NZ if step_y == 1 else column >= plane - NZ
                value = jnp.where(outside, 0.0, value)
            if step_x != 0:
                index = lax.broadcasted_iota(jnp.int32, (extent_x, plane), 0)
                value = jnp.where(index == (0 if step_x == 1 else extent_x - 1), 0.0, value)
            fbuf[q] = value

    for it in range(ITERS):
        last = it == ITERS - 1

        def send(found):
            for can_send, copy in found:
                if can_send is None:
                    copy.start()
                else:
                    pl.when(can_send)(copy.start)

        for sy in (1, -1):
            for rg, t in stages[sy]:
                collide(rg, t, it == 0)
            send(corner_copies(it, sy))
            send(tile_copies(it, sy))
        for rg, t in stages[0]:
            collide(rg, t, it == 0)
        send(row_copies(it))
        for rg, t in stages[None]:
            collide(rg, t, it == 0)
        pass_on()
        gather_moments()
        settle(it, False)
        values = halo_values(it)
        halo_moments(values)
        find_velocity(last)
        if not last:
            halo_populations(values)
        if not last:
            built = []
            for k in range(n_xsec):
                now = move(it, k, planes[k])
                for c in range(3):
                    current[k, c] = now[c]
                built.append(
                    build(it + 1, k, now, [pltpu.roll(arrived[order[k], c], 1, 0) for c in range(3)])
                )
            planes = [flat for _, flat in built]
            add_force(
                spread(
                    jnp.concatenate([sides for sides, _ in built], axis=1),
                    jnp.concatenate(planes, axis=1),
                ),
                True,
            )
            settle(it, True)

    for k in range(n_xsec - 1, -1, -1):
        now = move(ITERS - 1, k, planes[k])
        moved = [now[c] - arrived[order[k], c] for c in range(3)]
        ret_out[k, 0] = jnp.where(odd_row, moved[0], pltpu.roll(moved[1], 7, 0))
        ret_out[k, 1] = moved[2]
        if k > 0:
            transfer(ret_out.at[k], ret_in, out_sem.at[1], ret_recv, k).start()
    halo_populations(halo_values(ITERS - 1))
    totals = [jnp.zeros((8, LANES), jnp.float32) for _ in range(3)]
    for k in range(n_xsec):
        if k > 0:
            arrival(ret_in, out_sem.at[1], ret_recv, k).wait_recv()
        found = [ret_out[0, i] if k == 0 else ret_in[order[k], i] for i in range(2)]
        for j in range(capacity):
            here = place == order[k] * capacity + j
            for c in range(3):
                at = 2 * j + (0 if c == 1 else 1)
                value = found[c // 2][at:at + 1]
                totals[c] = jnp.where(here, spread_row(value), totals[c])
    for c in range(3):
        disp[c] = totals[c][0:owned]
    for i, ref in enumerate((outgoing, ret_out)):
        whole = ref.at[pl.ds(0, n_xsec - 1)]
        pltpu.make_async_copy(whole, whole, out_sem.at[i]).wait()
    settle(ITERS - 1, True)


CHUNKS = 1


def hand_over(evolved_in, moved_in, evolved, moved, out_sem):
    size = -(-Q // CHUNKS)
    stores = [pltpu.make_async_copy(moved_in, moved, out_sem.at[CHUNKS])]
    for i, first in enumerate(range(0, Q, size)):
        part = pl.ds(first, min(size, Q - first))
        stores.append(
            pltpu.make_async_copy(evolved_in.at[part], evolved.at[part], out_sem.at[i])
        )
    for store in stores:
        store.start()
    for store in stores:
        store.wait()


def per_device(n_vessel, n_xsec, populations, wall_flags, positions, vertex_rest_shift, home_brick):
    owned = positions.shape[0]
    capacity = max(2, 2 * owned // n_xsec)
    slots = n_xsec * capacity
    extent_x, plane = populations.shape[1:]
    f32 = jnp.float32
    vmem = pl.BlockSpec(memory_space=pltpu.VMEM)
    hbm = pl.BlockSpec(memory_space=pltpu.HBM)
    dma = pltpu.SemaphoreType.DMA
    evolved, moved = pl.pallas_call(
        functools.partial(kernel, n_vessel, n_xsec, capacity, extent_x, plane),
        out_shape=(
            pltpu.VMEM(populations.shape, f32),
            pltpu.VMEM((3, owned, LANES), f32),
        ),
        in_specs=[hbm] * 5,
        out_specs=(vmem, vmem),
        scratch_shapes=[
            pltpu.VMEM((extent_x, plane), jnp.int32),
            pltpu.VMEM((2, 3, owned, LANES), f32),
            pltpu.SMEM((1, owned), jnp.int32),
            pltpu.VMEM((Q, extent_x, plane), f32),
            pltpu.VMEM((4, extent_x, plane), f32),
            pltpu.VMEM((extent_x, plane), f32),
            pltpu.VMEM((3, extent_x, plane), f32),
            pltpu.VMEM((plane // LANES, 3 * extent_x, LANES), jnp.bfloat16),
            pltpu.VMEM((n_xsec, 3, 8, LANES), f32),
            pltpu.VMEM((n_xsec, 3, 8, LANES), f32),
            pltpu.VMEM((n_xsec, 3, 8, LANES), f32),
            pltpu.VMEM((n_xsec, 2, 8, LANES), f32),
            pltpu.VMEM((n_xsec, 2, 8, LANES), f32),
            pltpu.VMEM((ITERS, slots, extent_x, LANES), f32),
            pltpu.VMEM((ITERS, 2, len(X_DIRS[1]), plane), f32),
            pltpu.VMEM((ITERS, 2, len(X_DIRS[1]), plane), f32),
            pltpu.VMEM((ITERS, 2, extent_x + 8, LANES), f32),
            pltpu.VMEM((ITERS, 2, extent_x + 8, LANES), f32),
            pltpu.VMEM((ITERS, len(CORNERS), 8, LANES), f32),
            dma((4,)),
            dma((2,)),
            dma((n_xsec - 1,)),
            dma((n_xsec - 1,)),
            dma((ITERS, 3)),
            dma((ITERS, 3)),
        ],
        compiler_params=pltpu.CompilerParams(
            collective_id=0, has_side_effects=True, vmem_limit_bytes=40 << 20
        ),
    )(
        *(
            pltpu.with_memory_space_constraint(value, pltpu.HBM)
            for value in (
                populations,
                wall_flags,
                jnp.transpose(positions, (1, 0, 2)),
                jnp.transpose(vertex_rest_shift, (1, 0, 2)),
                jnp.transpose(home_brick),
            )
        )
    )
    evolved, moved = pl.pallas_call(
        hand_over,
        out_shape=(
            jax.ShapeDtypeStruct(evolved.shape, f32),
            jax.ShapeDtypeStruct(moved.shape, f32),
        ),
        in_specs=[vmem, vmem],
        out_specs=(hbm, hbm),
        scratch_shapes=[dma((CHUNKS + 1,))],
        compiler_params=pltpu.CompilerParams(vmem_limit_bytes=1 << 20),
    )(
        pltpu.with_memory_space_constraint(evolved, pltpu.VMEM),
        pltpu.with_memory_space_constraint(moved, pltpu.VMEM),
    )
    return evolved, jnp.transpose(moved, (1, 0, 2))


def solution(mesh):
    in_specs = (
        P(None, "vessel", "xsec"),
        P("vessel", "xsec"),
        P(("vessel", "xsec"), None, None),
        P(("vessel", "xsec"), None, None),
        P(("vessel", "xsec"), None),
    )
    out_specs = (P(None, "vessel", "xsec"), P(("vessel", "xsec"), None, None))
    return jax.shard_map(
        functools.partial(per_device, mesh.shape["vessel"], mesh.shape["xsec"]),
        mesh=mesh,
        in_specs=in_specs,
        out_specs=out_specs,
        check_vma=False,
    )
```

```python
import functools

import jax
import jax.numpy as jnp
from jax import lax
from jax.experimental import pallas as pl
from jax.experimental.pallas import tpu as pltpu
from jax.sharding import PartitionSpec as P

NZ = 32
ITERS = 2
LATTICE = [
    [0, 0, 0],
    [1, 0, 0],
    [-1, 0, 0],
    [0, 1, 0],
    [0, -1, 0],
    [0, 0, 1],
    [0, 0, -1],
    [1, 1, 0],
    [-1, -1, 0],
    [1, -1, 0],
    [-1, 1, 0],
    [1, 0, 1],
    [-1, 0, -1],
    [1, 0, -1],
    [-1, 0, 1],
    [0, 1, 1],
    [0, -1, -1],
    [0, 1, -1],
    [0, -1, 1],
]
Q = len(LATTICE)
OPPOSITE = [0, 2, 1, 4, 3, 6, 5, 8, 7, 10, 9, 12, 11, 14, 13, 16, 15, 18, 17]
WEIGHTS = [1.0 / 3.0] + [1.0 / 18.0] * 6 + [1.0 / 36.0] * 12
RELAX_TIME = 0.8
SPRING = 0.1
LANES = 128
GROUPS = LANES // NZ
FAR = -8.0
MESH = pl.DeviceIdType.MESH
X_DIRS = {s: [q for q in range(Q) if LATTICE[q][0] == s] for s in (1, -1)}
Y_DIRS = {s: [q for q in range(Q) if LATTICE[q][1] == s] for s in (1, -1)}
CORNERS = [q for q in range(Q) if LATTICE[q][0] != 0 and LATTICE[q][1] != 0]


def signed_sum(terms):
    total = None
    for sign, value in terms:
        if total is None:
            total = value if sign > 0 else -value
        else:
            total = total + value if sign > 0 else total - value
    return total


def tree_sum(terms):
    while len(terms) > 1:
        terms = [
            terms[i] + terms[i + 1] if i + 1 < len(terms) else terms[i]
            for i in range(0, len(terms), 2)
        ]
    return terms[0]


def moments(fs):
    both = [fs[q] + fs[OPPOSITE[q]] for q in range(1, Q, 2)]
    flow = {q: fs[q] - fs[OPPOSITE[q]] for q in range(1, Q, 2)}
    density = tree_sum([fs[0]] + both)
    momentum = []
    for d in range(3):
        plus = tree_sum([flow[q] for q in flow if LATTICE[q][d] == 1])
        minus = [flow[q] for q in flow if LATTICE[q][d] == -1]
        momentum.append(plus - tree_sum(minus) if minus else plus)
    return density, momentum


def peers_by_distance(h, n):
    near = jnp.minimum(h, n - 1 - h)
    toward = jnp.where(h < n - 1 - h, 1, -1)
    order = [h]
    for k in range(1, n):
        step = (k + 1) // 2
        paired = h + step if k % 2 else h - step
        order.append(jnp.where(k <= 2 * near, paired, h + toward * (k - near)))
    return order


def kernel(
    n_vessel, n_xsec, capacity, extent_x, plane,
    pop_hbm, wall_hbm, pos_hbm, shift_hbm, home_hbm, fbuf, disp,
    wall, points, home, rbuf, mom, scale, force, vel,
    outgoing, arrived, current, ret_out, ret_in, wxs,
    xs_out, xs_in, ys_out, ys_in, cs_in, meter,
    load_sem, out_sem, a2a_recv, ret_recv, halo_recv,
):
    v = lax.axis_index("vessel")
    h = lax.axis_index("xsec")
    v_side = {1: lax.rem(v + 1, n_vessel), -1: lax.rem(v + n_vessel - 1, n_vessel)}
    owned = points.shape[2]
    pos, shift = points.at[0], points.at[1]
    extent_y = plane // NZ
    tiles = plane // LANES
    row_groups = extent_x // 8
    order = peers_by_distance(h, n_xsec)
    has_side = {1: h < n_xsec - 1, -1: h > 0}

    barrier = pltpu.get_barrier_semaphore()
    for k in range(n_xsec - 1, 0, -1):
        pl.semaphore_signal(barrier, inc=1, device_id=(v, order[k]), device_id_type=MESH)
    for sx in (1, -1):
        pl.semaphore_signal(barrier, inc=1, device_id=(v_side[sx], h), device_id_type=MESH)
    small_loads = [
        pltpu.make_async_copy(source, target, load_sem.at[i])
        for i, source, target in ((0, pos_hbm, pos), (0, shift_hbm, shift), (1, home_hbm, home))
    ]
    for copy in small_loads:
        copy.start()
    load = pltpu.make_async_copy(pop_hbm, fbuf, load_sem.at[2])
    load.start()
    load_wall = pltpu.make_async_copy(wall_hbm, wall, load_sem.at[2])
    load_wall.start()
    xs_out[...] = jnp.zeros(xs_out.shape, jnp.float32)

    for sy in (1, -1):

        @pl.when(jnp.logical_not(has_side[sy]))
        def _(sy=sy):
            side = 0 if sy == -1 else 1
            for it in range(ITERS):
                ys_in[it, side] = jnp.zeros(ys_in.shape[2:], jnp.float32)
                for k, q in enumerate(CORNERS):
                    if LATTICE[q][1] == -sy:
                        cs_in[it, k] = jnp.zeros((8, LANES), jnp.float32)

    pltpu.make_async_copy(points, points, load_sem.at[0]).wait()
    small_loads[2].wait()

    row = lax.broadcasted_iota(jnp.int32, (8, LANES), 0)
    odd_row = (row & 1) == 1
    slot_row = row >> 1
    homes = [home[0, o] for o in range(owned)]
    ranks = []
    for o in range(owned):
        rank = jnp.int32(0)
        for p in range(o):
            rank = rank + (homes[p] == homes[o]).astype(jnp.int32)
        ranks.append(rank)

    def spread_row(value, rows=8):
        return jnp.broadcast_to(value, (rows, LANES))

    sources = []
    for c in range(3):
        sources.append([])
        for o in range(owned):
            start = spread_row(pos[c, o:o + 1, :])
            rest = start + spread_row(shift[c, o:o + 1, :])
            sources[c].append(jnp.where(odd_row, start, rest))
    for p in range(n_xsec):
        chosen = [slot_row == jnp.where(homes[o] == p, ranks[o], 8) for o in range(owned)]
        for c in range(3):
            total = jnp.full((8, LANES), FAR, jnp.float32)
            for o in range(owned):
                total = jnp.where(chosen[o], sources[c][o], total)
            outgoing[p, c] = total
    place = jnp.full((8, LANES), -1, jnp.int32)
    for o in range(owned):
        place = jnp.where(row == o, homes[o] * capacity + ranks[o], place)

    pl.semaphore_wait(barrier, n_xsec + 1)

    def settle_blocks(ref, i):
        whole = ref.at[pl.ds(0, n_xsec - 1)]
        pltpu.make_async_copy(whole, whole, out_sem.at[i]).wait()

    def slot_of(sender, receiver):
        return lax.rem(sender - receiver + n_xsec - 1, n_xsec)

    def transfer(source, target, send, recv, k):
        return pltpu.make_async_remote_copy(
            src_ref=source,
            dst_ref=target.at[h],
            send_sem=send,
            recv_sem=recv.at[slot_of(h, order[k])],
            device_id=(v, order[k]),
            device_id_type=MESH,
        )

    def arrival(target, send, recv, k):
        return pltpu.make_async_remote_copy(
            src_ref=target.at[order[k]],
            dst_ref=target.at[order[k]],
            send_sem=send,
            recv_sem=recv.at[slot_of(order[k], h)],
            device_id=(v, order[k]),
            device_id_type=MESH,
        )

    outbound = [
        transfer(outgoing.at[order[k]], arrived, out_sem.at[0], a2a_recv, k)
        for k in range(n_xsec - 1, 0, -1)
    ]
    for copy in outbound:
        copy.start()
    arrived[h] = outgoing[h]

    gain = 1.0 / RELAX_TIME

    def blocks_of(height):
        return [
            (pl.ds(r, height), pl.ds(t * LANES, LANES))
            for t in range(tiles)
            for r in range(0, extent_x, height)
        ]

    def prepare():
        for rows, lanes in blocks_of(8):
            fs = [fbuf[q, rows, lanes] for q in range(Q)]
            density, momentum = moments(fs)
            solid = wall[rows, lanes] == 1
            inverse = 1.0 / density
            mom[0, rows, lanes] = jnp.where(solid, 0.0, density)
            for d in range(3):
                mom[1 + d, rows, lanes] = momentum[d] * inverse
            scale[rows, lanes] = RELAX_TIME * inverse
            for q in range(Q):
                fbuf[q, rows, lanes] = jnp.where(solid, fs[OPPOSITE[q]], (1.0 - gain) * fs[q])

    def gather_moments():
        for rows, lanes in blocks_of(8):
            density, momentum = moments([fbuf[q, rows, lanes] for q in range(Q)])
            mom[0, rows, lanes] = density
            for d in range(3):
                mom[1 + d, rows, lanes] = momentum[d]

    def find_velocity(last):
        for rows, lanes in blocks_of(16):
            density = mom[0, rows, lanes]
            inverse = 1.0 / density
            half = 0.5 * inverse
            for d in range(3):
                moved = mom[1 + d, rows, lanes] * inverse
                value = moved + half * force[d, rows, lanes]
                vel[lanes.start // LANES, pl.ds(d * extent_x + rows.start, 16)] = value.astype(
                    jnp.bfloat16
                )
                if not last:
                    mom[1 + d, rows, lanes] = moved
            if not last:
                mom[0, rows, lanes] = jnp.where(wall[rows, lanes] == 1, 0.0, density)
                scale[rows, lanes] = RELAX_TIME * inverse

    def collide(rg, t, prepared):
        rows = pl.ds(rg * 8, 8)
        lanes = pl.ds(t * LANES, LANES)
        density = mom[0, rows, lanes]
        factor = scale[rows, lanes]
        u = [mom[1 + d, rows, lanes] + factor * force[d, rows, lanes] for d in range(3)]
        square = u[0] * u[0] + u[1] * u[1] + u[2] * u[2]
        part = density * (1.0 - 1.5 * square)
        bases = {w: (gain * w) * part for w in sorted(set(WEIGHTS))}
        twice = {w: (2.0 * gain * w) * density for w in sorted(set(WEIGHTS))}
        half = [1.5 * component for component in u]

        solid = None if prepared else wall[rows, lanes] == 1

        def write(q, own, other, change):
            if prepared:
                rbuf[q, rows, lanes] = own + change
            else:
                rbuf[q, rows, lanes] = jnp.where(solid, other, own * (1.0 - gain) + change)

        f0 = fbuf[0, rows, lanes]
        write(0, f0, f0, bases[WEIGHTS[0]])
        for q in range(1, Q, 2):
            o = OPPOSITE[q]
            along = signed_sum(
                [(LATTICE[q][d], half[d]) for d in range(3) if LATTICE[q][d] != 0]
            )
            fq = fbuf[q, rows, lanes]
            fo = fbuf[o, rows, lanes]
            odd = twice[WEIGHTS[q]] * along
            even = bases[WEIGHTS[q]] + odd * along
            write(q, fq, fo, even + odd)
            write(o, fo, fq, even - odd)

    cell_x = lax.broadcasted_iota(jnp.int32, (extent_x, LANES), 0).astype(jnp.float32)
    cell_y = lax.broadcasted_iota(jnp.int32, (max(8, extent_y), LANES), 0).astype(jnp.float32)
    cell_z = lax.broadcasted_iota(jnp.int32, (NZ, LANES), 0).astype(jnp.float32)

    def hat(coordinate, cells):
        return jnp.maximum(0.0, 1.0 - jnp.abs(coordinate - cells))

    def build(it, k, now, fixed):
        pulls = [SPRING * (fixed[c] - now[c]) for c in range(3)]
        sides, planes = [], []
        for j in range(capacity):
            at = slice(2 * j + 1, 2 * j + 2)
            wx = hat(now[0][at], cell_x)
            wy = hat(now[1][at], cell_y)
            wz = hat(now[2][at], cell_z)
            wxs[it, k * capacity + j] = wx
            flat = jnp.concatenate([wy[y:y + 1] * wz for y in range(extent_y)], axis=0)
            planes.append(flat.astype(jnp.bfloat16))
            side = jnp.concatenate([pulls[c][at] * wx for c in range(3)], axis=0)
            sides.append(side.astype(jnp.bfloat16))
        return jnp.concatenate(sides, axis=1), jnp.concatenate(planes, axis=1)

    def spread(sides, planes):
        return lax.dot_general(
            sides, planes, (((1,), (1,)), ((), ())), preferred_element_type=jnp.float32
        )

    def spread_t(sides, planes):
        field = lax.dot_general(
            planes, sides, (((1,), (1,)), ((), ())), preferred_element_type=jnp.float32
        )
        field = jnp.concatenate([field, jnp.zeros((plane, LANES - 3 * extent_x), jnp.float32)], axis=1)
        return jnp.transpose(field)[0:3 * extent_x]

    def add_force(field, first):
        for d in range(3):
            part = field[d * extent_x:(d + 1) * extent_x]
            force[d] = part if first else force[d] + part

    low_rows = row < 4
    mid_rows = jnp.logical_and(row >= 2, row < 6)
    second = (row & 2) != 0

    def merge(mask, a, b, shift):
        return jnp.where(mask, a, b) + pltpu.roll(jnp.where(mask, b, a), shift, 0)

    def row_sums(parts):
        parts = parts + [jnp.zeros((8, LANES), jnp.float32)] * (4 - len(parts))
        pairs = merge(low_rows, parts[1], parts[3], 4), merge(mid_rows, parts[2], parts[0], 4)
        total = merge(second, pairs[0], pairs[1], 2)
        return total + pltpu.roll(total, 1, 0)

    def move(it, k, planes):
        flow = jnp.concatenate([vel[t] for t in range(tiles)], axis=1)
        sampled = jnp.dot(flow, planes, preferred_element_type=jnp.float32)
        result = []
        for c in range(3):
            parts = []
            for j in range(capacity):
                part = sampled[c * extent_x:(c + 1) * extent_x, j * LANES:(j + 1) * LANES]
                part = part * wxs[it, k * capacity + j]
                parts.append(tree_sum([part[i:i + 8] for i in range(0, extent_x, 8)]))
            result.append(current[k, c] + row_sums(parts))
        return result

    pltpu.make_async_copy(rbuf, rbuf, load_sem.at[2]).wait()
    prepare()
    planes = []
    for k in range(n_xsec):
        if k > 0:
            arrival(arrived, out_sem.at[0], a2a_recv, k).wait_recv()
        now = [arrived[order[k], c] for c in range(3)]
        for c in range(3):
            current[k, c] = now[c]
        sides, flat = build(0, k, now, [pltpu.roll(now[c], 1, 0) for c in range(3)])
        planes.append(flat)
        add_force(spread(sides, flat), k == 0)

    settle_blocks(outgoing, 0)

    depth = lax.broadcasted_iota(jnp.int32, (extent_x, plane), 1) % NZ
    lane = lax.broadcasted_iota(jnp.int32, (extent_x, LANES), 1)
    line = lax.broadcasted_iota(jnp.int32, (1, plane), 1)

    def shift_x(value, step_x, edge):
        rolled = pltpu.roll(value, step_x % extent_x, 0)
        index = lax.broadcasted_iota(jnp.int32, value.shape, 0)
        enters = index == (0 if step_x == 1 else extent_x - 1)
        return jnp.where(enters, jnp.broadcast_to(edge, value.shape), rolled)

    last_tile = pl.ds(plane - LANES, LANES)
    first_tile = pl.ds(0, LANES)

    def halo_rows(it):
        for side, sx in enumerate((1, -1)):
            found = []
            for k, q in enumerate(X_DIRS[sx]):
                _, sy, sz = LATTICE[q]
                amount = sy * NZ + sz
                value = xs_in[it, side, k:k + 1, :]
                if amount != 0:
                    value = pltpu.roll(
                        jnp.broadcast_to(value, (8, plane)), amount % plane, 1
                    )[0:1]
                if sz != 0:
                    value = jnp.where(depth[0:1] == (0 if sz == 1 else NZ - 1), 0.0, value)
                if sy != 0:
                    outside = line < NZ if sy == 1 else line >= plane - NZ
                    value = jnp.where(outside, 0.0, value)
                found.append((q, value))
            yield (0 if sx == 1 else extent_x - 1), found

    def halo_tiles(it):
        for side, sy in enumerate((1, -1)):
            origin = LANES - NZ if sy == 1 else 0
            enters = lane < NZ if sy == 1 else lane >= LANES - NZ
            found = []
            for g, q in enumerate(Y_DIRS[sy]):
                sx, _, sz = LATTICE[q]
                amount = sy * NZ + sz
                finish = origin + amount
                if g < GROUPS:
                    value = pltpu.roll(
                        ys_in[it, side, 0:extent_x, :], (finish - g * NZ) % LANES, 1
                    )
                else:
                    folded = ys_in[it, side, extent_x:extent_x + 8, :]
                    value = jnp.concatenate(
                        [
                            pltpu.roll(folded, (finish - r * NZ) % LANES, 1)
                            for r in range(row_groups)
                        ],
                        axis=0,
                    )
                if sx != 0:
                    corner = pltpu.roll(cs_in[it, CORNERS.index(q)], amount % LANES, 1)
                    value = shift_x(value, sx, corner[7:8] if sx == 1 else corner[0:1])
                keep = enters
                if sz != 0:
                    keep = jnp.logical_and(enters, lane % NZ != (0 if sz == 1 else NZ - 1))
                found.append((q, jnp.where(keep, value, 0.0)))
            yield (first_tile if sy == 1 else last_tile), found

    def add_moments(found, where):
        mom[(0, *where)] = mom[(0, *where)] + tree_sum([value for _, value in found])
        for d in range(3):
            terms = [(LATTICE[q][d], value) for q, value in found if LATTICE[q][d] != 0]
            mom[(1 + d, *where)] = mom[(1 + d, *where)] + signed_sum(
                sorted(terms, key=lambda term: -term[0])
            )

    def halo_values(it):
        return list(halo_rows(it)), list(halo_tiles(it))

    def halo_moments(values):
        for edge, found in values[0]:
            add_moments(found, (slice(edge, edge + 1), slice(None)))
        for tile, found in values[1]:
            add_moments(found, (slice(None), tile))

    def halo_populations(values):
        for edge, found in values[0]:
            for q, value in found:
                fbuf[q, edge:edge + 1, :] = value
        for tile, found in values[1]:
            for q, value in found:
                fbuf[q, :, tile] = fbuf[q, :, tile] + value

    group = lax.broadcasted_iota(jnp.int32, (extent_x, LANES), 1) // NZ
    group8 = lax.broadcasted_iota(jnp.int32, (8, LANES), 1) // NZ
    edge_groups = sorted({0, row_groups - 1})
    side_tiles = {1: tiles - 1, -1: 0}
    stages = {1: [], -1: [], 0: [], None: []}
    for rg in range(row_groups):
        for t in range(tiles):
            if t == side_tiles[1]:
                stages[1].append((rg, t))
            elif t == side_tiles[-1]:
                stages[-1].append((rg, t))
            elif rg in edge_groups:
                stages[0].append((rg, t))
            else:
                stages[None].append((rg, t))

    def corner_copies(it, side):
        for k, q in enumerate(CORNERS):
            sx, sy, _ = LATTICE[q]
            if sy != side:
                continue
            copy = pltpu.make_async_remote_copy(
                src_ref=rbuf.at[
                    q,
                    pl.ds(extent_x - 8 if sx == 1 else 0, 8),
                    last_tile if sy == 1 else first_tile,
                ],
                dst_ref=cs_in.at[it, k],
                send_sem=out_sem.at[0],
                recv_sem=halo_recv.at[it],
                device_id=(v_side[sx], h + sy),
                device_id_type=MESH,
            )
            yield has_side[sy], copy

    def row_copies(it):
        for side, sx in enumerate((1, -1)):
            edge = extent_x - 1 if sx == 1 else 0
            for k, q in enumerate(X_DIRS[sx]):
                xs_out[it, side, k:k + 1, :] = rbuf[q, edge:edge + 1, :]
            yield None, pltpu.make_async_remote_copy(
                src_ref=xs_out.at[it, side],
                dst_ref=xs_in.at[it, side],
                send_sem=out_sem.at[0],
                recv_sem=halo_recv.at[it],
                device_id=(v_side[sx], h),
                device_id_type=MESH,
            )

    def tile_copies(it, sy):
        for side in (0,) if sy == 1 else (1,):
            tile = last_tile if sy == 1 else first_tile
            origin = LANES - NZ if sy == 1 else 0
            dirs = Y_DIRS[sy]
            packed = None
            for g in range(GROUPS):
                part = pltpu.roll(rbuf[dirs[g], :, tile], (g * NZ - origin) % LANES, 1)
                packed = part if packed is None else jnp.where(group == g, part, packed)
            ys_out[it, side, 0:extent_x, :] = packed
            packed = None
            for g in range(row_groups):
                part = pltpu.roll(
                    rbuf[dirs[GROUPS], g * 8:(g + 1) * 8, tile], (g * NZ - origin) % LANES, 1
                )
                packed = part if packed is None else jnp.where(group8 == g, part, packed)
            ys_out[it, side, extent_x:extent_x + 8, :] = packed
            yield has_side[sy], pltpu.make_async_remote_copy(
                src_ref=ys_out.at[it, side],
                dst_ref=ys_in.at[it, side],
                send_sem=out_sem.at[0],
                recv_sem=halo_recv.at[it],
                device_id=(v, h + sy),
                device_id_type=MESH,
            )

    def settle(sem):
        side = row_groups + 1 + len(CORNERS) // 2
        between = jnp.logical_and(has_side[1], has_side[-1])
        most = meter.at[pl.ds(0, 2 * tiles + 2 * side)]
        some = meter.at[pl.ds(0, 2 * tiles + side)]
        pl.when(between)(pltpu.make_async_copy(most, most, sem).wait)
        pl.when(jnp.logical_not(between))(pltpu.make_async_copy(some, some, sem).wait)

    def pass_on():
        for q in range(Q):
            step_x, step_y, step_z = LATTICE[q]
            value = rbuf[q]
            if step_x != 0:
                value = pltpu.roll(value, step_x % extent_x, 0)
            amount = step_y * NZ + step_z
            if amount != 0:
                value = pltpu.roll(value, amount % plane, 1)
            if step_z != 0:
                value = jnp.where(depth == (0 if step_z == 1 else NZ - 1), 0.0, value)
            if step_y != 0:
                column = lax.broadcasted_iota(jnp.int32, (extent_x, plane), 1)
                outside = column < NZ if step_y == 1 else column >= plane - NZ
                value = jnp.where(outside, 0.0, value)
            if step_x != 0:
                index = lax.broadcasted_iota(jnp.int32, (extent_x, plane), 0)
                value = jnp.where(index == (0 if step_x == 1 else extent_x - 1), 0.0, value)
            fbuf[q] = value

    for it in range(ITERS):
        last = it == ITERS - 1

        def send(found):
            for can_send, copy in found:
                if can_send is None:
                    copy.start()
                else:
                    pl.when(can_send)(copy.start)

        for sy in (1, -1):
            for rg, t in stages[sy]:
                collide(rg, t, it == 0)
            send(corner_copies(it, sy))
            send(tile_copies(it, sy))
        for rg, t in stages[0]:
            collide(rg, t, it == 0)
        send(row_copies(it))
        for rg, t in stages[None]:
            collide(rg, t, it == 0)
        pass_on()
        gather_moments()
        settle(halo_recv.at[it])
        values = halo_values(it)
        halo_moments(values)
        find_velocity(last)
        if not last:
            halo_populations(values)
            built = []
            for k in range(n_xsec):
                now = move(it, k, planes[k])
                for c in range(3):
                    current[k, c] = now[c]
                built.append(
                    build(it + 1, k, now, [pltpu.roll(arrived[order[k], c], 1, 0) for c in range(3)])
                )
            planes = [flat for _, flat in built]
            add_force(
                spread(
                    jnp.concatenate([sides for sides, _ in built], axis=1),
                    jnp.concatenate(planes, axis=1),
                ),
                True,
            )
            settle(out_sem.at[0])

    for k in range(n_xsec - 1, -1, -1):
        now = move(ITERS - 1, k, planes[k])
        moved = [now[c] - arrived[order[k], c] for c in range(3)]
        ret_out[k, 0] = jnp.where(odd_row, moved[0], pltpu.roll(moved[1], 7, 0))
        ret_out[k, 1] = moved[2]
        if k > 0:
            transfer(ret_out.at[k], ret_in, out_sem.at[1], ret_recv, k).start()
    halo_populations(halo_values(ITERS - 1))
    settle(out_sem.at[0])
    settle_blocks(ret_out, 1)
    totals = [jnp.zeros((8, LANES), jnp.float32) for _ in range(3)]
    for k in range(n_xsec):
        if k > 0:
            arrival(ret_in, out_sem.at[1], ret_recv, k).wait_recv()
        found = [ret_out[0, i] if k == 0 else ret_in[order[k], i] for i in range(2)]
        for j in range(capacity):
            here = place == order[k] * capacity + j
            for c in range(3):
                at = 2 * j + (0 if c == 1 else 1)
                value = found[c // 2][at:at + 1]
                totals[c] = jnp.where(here, spread_row(value), totals[c])
    for c in range(3):
        disp[c] = totals[c][0:owned]


CHUNKS = 1


def hand_over(evolved_in, moved_in, evolved, moved, out_sem):
    size = -(-Q // CHUNKS)
    stores = [pltpu.make_async_copy(moved_in, moved, out_sem.at[CHUNKS])]
    for i, first in enumerate(range(0, Q, size)):
        part = pl.ds(first, min(size, Q - first))
        stores.append(
            pltpu.make_async_copy(evolved_in.at[part], evolved.at[part], out_sem.at[i])
        )
    for store in stores:
        store.start()
    for store in stores:
        store.wait()


def per_device(n_vessel, n_xsec, populations, wall_flags, positions, vertex_rest_shift, home_brick):
    owned = positions.shape[0]
    capacity = max(2, 2 * owned // n_xsec)
    slots = n_xsec * capacity
    extent_x, plane = populations.shape[1:]
    f32 = jnp.float32
    meters = 2 * (plane // LANES + extent_x // 8 + 1) + len(CORNERS)
    vmem = pl.BlockSpec(memory_space=pltpu.VMEM)
    hbm = pl.BlockSpec(memory_space=pltpu.HBM)
    dma = pltpu.SemaphoreType.DMA
    evolved, moved = pl.pallas_call(
        functools.partial(kernel, n_vessel, n_xsec, capacity, extent_x, plane),
        out_shape=(
            pltpu.VMEM(populations.shape, f32),
            pltpu.VMEM((3, owned, LANES), f32),
        ),
        in_specs=[hbm] * 5,
        out_specs=(vmem, vmem),
        scratch_shapes=[
            pltpu.VMEM((extent_x, plane), jnp.int32),
            pltpu.VMEM((2, 3, owned, LANES), f32),
            pltpu.SMEM((1, owned), jnp.int32),
            pltpu.VMEM((Q + 1, extent_x, plane), f32),
            pltpu.VMEM((4, extent_x, plane), f32),
            pltpu.VMEM((extent_x, plane), f32),
            pltpu.VMEM((3, extent_x, plane), f32),
            pltpu.VMEM((plane // LANES, 3 * extent_x, LANES), jnp.bfloat16),
            pltpu.VMEM((n_xsec, 3, 8, LANES), f32),
            pltpu.VMEM((n_xsec, 3, 8, LANES), f32),
            pltpu.VMEM((n_xsec, 3, 8, LANES), f32),
            pltpu.VMEM((n_xsec, 2, 8, LANES), f32),
            pltpu.VMEM((n_xsec, 2, 8, LANES), f32),
            pltpu.VMEM((ITERS, slots, extent_x, LANES), f32),
            pltpu.VMEM((ITERS, 2, 8, plane), f32),
            pltpu.VMEM((ITERS, 2, 8, plane), f32),
            pltpu.VMEM((ITERS, 2, extent_x + 8, LANES), f32),
            pltpu.VMEM((ITERS, 2, extent_x + 8, LANES), f32),
            pltpu.VMEM((ITERS, len(CORNERS), 8, LANES), f32),
            pltpu.VMEM((meters, 8, LANES), f32),
            dma((3,)),
            dma((2,)),
            dma((n_xsec - 1,)),
            dma((n_xsec - 1,)),
            dma((ITERS,)),
        ],
        compiler_params=pltpu.CompilerParams(
            collective_id=0, has_side_effects=True, vmem_limit_bytes=40 << 20
        ),
    )(
        *(
            pltpu.with_memory_space_constraint(value, pltpu.HBM)
            for value in (
                populations,
                wall_flags,
                jnp.transpose(positions, (1, 0, 2)),
                jnp.transpose(vertex_rest_shift, (1, 0, 2)),
                jnp.transpose(home_brick),
            )
        )
    )
    evolved, moved = pl.pallas_call(
        hand_over,
        out_shape=(
            jax.ShapeDtypeStruct(evolved.shape, f32),
            jax.ShapeDtypeStruct(moved.shape, f32),
        ),
        in_specs=[vmem, vmem],
        out_specs=(hbm, hbm),
        scratch_shapes=[dma((CHUNKS + 1,))],
        compiler_params=pltpu.CompilerParams(vmem_limit_bytes=1 << 20),
    )(
        pltpu.with_memory_space_constraint(evolved, pltpu.VMEM),
        pltpu.with_memory_space_constraint(moved, pltpu.VMEM),
    )
    return evolved, jnp.transpose(moved, (1, 0, 2))


def solution(mesh):
    in_specs = (
        P(None, "vessel", "xsec"),
        P("vessel", "xsec"),
        P(("vessel", "xsec"), None, None),
        P(("vessel", "xsec"), None, None),
        P(("vessel", "xsec"), None),
    )
    out_specs = (P(None, "vessel", "xsec"), P(("vessel", "xsec"), None, None))
    return jax.shard_map(
        functools.partial(per_device, mesh.shape["vessel"], mesh.shape["xsec"]),
        mesh=mesh,
        in_specs=in_specs,
        out_specs=out_specs,
        check_vma=False,
    )
```

```python
import functools

import jax
import jax.numpy as jnp
from jax import lax
from jax.experimental import pallas as pl
from jax.experimental.pallas import tpu as pltpu
from jax.sharding import PartitionSpec as P

NZ = 32
ITERS = 2
LATTICE = [
    [0, 0, 0],
    [1, 0, 0],
    [-1, 0, 0],
    [0, 1, 0],
    [0, -1, 0],
    [0, 0, 1],
    [0, 0, -1],
    [1, 1, 0],
    [-1, -1, 0],
    [1, -1, 0],
    [-1, 1, 0],
    [1, 0, 1],
    [-1, 0, -1],
    [1, 0, -1],
    [-1, 0, 1],
    [0, 1, 1],
    [0, -1, -1],
    [0, 1, -1],
    [0, -1, 1],
]
Q = len(LATTICE)
OPPOSITE = [0, 2, 1, 4, 3, 6, 5, 8, 7, 10, 9, 12, 11, 14, 13, 16, 15, 18, 17]
WEIGHTS = [1.0 / 3.0] + [1.0 / 18.0] * 6 + [1.0 / 36.0] * 12
RELAX_TIME = 0.8
SPRING = 0.1
LANES = 128
GROUPS = LANES // NZ
FAR = -8.0
MESH = pl.DeviceIdType.MESH
X_DIRS = {s: [q for q in range(Q) if LATTICE[q][0] == s] for s in (1, -1)}
Y_DIRS = {s: [q for q in range(Q) if LATTICE[q][1] == s] for s in (1, -1)}
CORNERS = [q for q in range(Q) if LATTICE[q][0] != 0 and LATTICE[q][1] != 0]


def signed_sum(terms):
    total = None
    for sign, value in terms:
        if total is None:
            total = value if sign > 0 else -value
        else:
            total = total + value if sign > 0 else total - value
    return total


def tree_sum(terms):
    while len(terms) > 1:
        terms = [
            terms[i] + terms[i + 1] if i + 1 < len(terms) else terms[i]
            for i in range(0, len(terms), 2)
        ]
    return terms[0]


def moments(fs):
    both = [fs[q] + fs[OPPOSITE[q]] for q in range(1, Q, 2)]
    flow = {q: fs[q] - fs[OPPOSITE[q]] for q in range(1, Q, 2)}
    density = tree_sum([fs[0]] + both)
    momentum = []
    for d in range(3):
        plus = tree_sum([flow[q] for q in flow if LATTICE[q][d] == 1])
        minus = [flow[q] for q in flow if LATTICE[q][d] == -1]
        momentum.append(plus - tree_sum(minus) if minus else plus)
    return density, momentum


def peers_by_distance(h, n):
    near = jnp.minimum(h, n - 1 - h)
    toward = jnp.where(h < n - 1 - h, 1, -1)
    order = [h]
    for k in range(1, n):
        step = (k + 1) // 2
        paired = h + step if k % 2 else h - step
        order.append(jnp.where(k <= 2 * near, paired, h + toward * (k - near)))
    return order


def kernel(
    n_vessel, n_xsec, capacity, extent_x, plane,
    pop_hbm, wall_hbm, pos_hbm, shift_hbm, home_hbm, fbuf, disp,
    wall, points, home, rbuf, mom, scale, force, vel,
    outgoing, arrived, current, ret_out, ret_in, wxs,
    xs_out, xs_in, ys_out, ys_in, cs_in, meter,
    load_sem, out_sem, a2a_recv, ret_recv, halo_recv,
):
    v = lax.axis_index("vessel")
    h = lax.axis_index("xsec")
    v_side = {1: lax.rem(v + 1, n_vessel), -1: lax.rem(v + n_vessel - 1, n_vessel)}
    owned = points.shape[2]
    pos, shift = points.at[0], points.at[1]
    extent_y = plane // NZ
    tiles = plane // LANES
    row_groups = extent_x // 8
    order = peers_by_distance(h, n_xsec)
    has_side = {1: h < n_xsec - 1, -1: h > 0}

    barrier = pltpu.get_barrier_semaphore()
    for k in range(n_xsec - 1, 0, -1):
        pl.semaphore_signal(barrier, inc=1, device_id=(v, order[k]), device_id_type=MESH)
    for sx in (1, -1):
        pl.semaphore_signal(barrier, inc=1, device_id=(v_side[sx], h), device_id_type=MESH)
    small_loads = [
        pltpu.make_async_copy(source, target, load_sem.at[i])
        for i, source, target in ((0, pos_hbm, pos), (0, shift_hbm, shift), (1, home_hbm, home))
    ]
    for copy in small_loads:
        copy.start()
    xs_out[...] = jnp.zeros(xs_out.shape, jnp.float32)

    for sy in (1, -1):

        @pl.when(jnp.logical_not(has_side[sy]))
        def _(sy=sy):
            side = 0 if sy == -1 else 1
            for it in range(ITERS):
                ys_in[it, side] = jnp.zeros(ys_in.shape[2:], jnp.float32)
                for k, q in enumerate(CORNERS):
                    if LATTICE[q][1] == -sy:
                        cs_in[it, k] = jnp.zeros((8, LANES), jnp.float32)

    pltpu.make_async_copy(points, points, load_sem.at[0]).wait()
    small_loads[2].wait()
    load = pltpu.make_async_copy(pop_hbm, fbuf, load_sem.at[2])
    load.start()
    load_wall = pltpu.make_async_copy(wall_hbm, wall, load_sem.at[2])
    load_wall.start()

    row = lax.broadcasted_iota(jnp.int32, (8, LANES), 0)
    odd_row = (row & 1) == 1
    slot_row = row >> 1
    homes = [home[0, o] for o in range(owned)]
    ranks = []
    for o in range(owned):
        rank = jnp.int32(0)
        for p in range(o):
            rank = rank + (homes[p] == homes[o]).astype(jnp.int32)
        ranks.append(rank)

    def spread_row(value, rows=8):
        return jnp.broadcast_to(value, (rows, LANES))

    sources = []
    for c in range(3):
        sources.append([])
        for o in range(owned):
            start = spread_row(pos[c, o:o + 1, :])
            rest = start + spread_row(shift[c, o:o + 1, :])
            sources[c].append(jnp.where(odd_row, start, rest))
    for p in range(n_xsec):
        chosen = [slot_row == jnp.where(homes[o] == p, ranks[o], 8) for o in range(owned)]
        for c in range(3):
            total = jnp.full((8, LANES), FAR, jnp.float32)
            for o in range(owned):
                total = jnp.where(chosen[o], sources[c][o], total)
            outgoing[p, c] = total
    place = jnp.full((8, LANES), -1, jnp.int32)
    for o in range(owned):
        place = jnp.where(row == o, homes[o] * capacity + ranks[o], place)

    pl.semaphore_wait(barrier, n_xsec + 1)

    def settle_blocks(ref, i):
        whole = ref.at[pl.ds(0, n_xsec - 1)]
        pltpu.make_async_copy(whole, whole, out_sem.at[i]).wait()

    def slot_of(sender, receiver):
        return lax.rem(sender - receiver + n_xsec - 1, n_xsec)

    def transfer(source, target, send, recv, k):
        return pltpu.make_async_remote_copy(
            src_ref=source,
            dst_ref=target.at[h],
            send_sem=send,
            recv_sem=recv.at[slot_of(h, order[k])],
            device_id=(v, order[k]),
            device_id_type=MESH,
        )

    def arrival(target, send, recv, k):
        return pltpu.make_async_remote_copy(
            src_ref=target.at[order[k]],
            dst_ref=target.at[order[k]],
            send_sem=send,
            recv_sem=recv.at[slot_of(order[k], h)],
            device_id=(v, order[k]),
            device_id_type=MESH,
        )

    outbound = [
        transfer(outgoing.at[order[k]], arrived, out_sem.at[0], a2a_recv, k)
        for k in range(n_xsec - 1, 0, -1)
    ]
    for copy in outbound:
        copy.start()
    arrived[h] = outgoing[h]

    gain = 1.0 / RELAX_TIME

    def blocks_of(height):
        return [
            (pl.ds(r, height), pl.ds(t * LANES, LANES))
            for t in range(tiles)
            for r in range(0, extent_x, height)
        ]

    def prepare():
        for rows, lanes in blocks_of(8):
            fs = [fbuf[q, rows, lanes] for q in range(Q)]
            density, momentum = moments(fs)
            solid = wall[rows, lanes] == 1
            inverse = 1.0 / density
            mom[0, rows, lanes] = jnp.where(solid, 0.0, density)
            for d in range(3):
                mom[1 + d, rows, lanes] = momentum[d] * inverse
            scale[rows, lanes] = RELAX_TIME * inverse
            for q in range(Q):
                fbuf[q, rows, lanes] = jnp.where(solid, fs[OPPOSITE[q]], (1.0 - gain) * fs[q])

    def gather_moments():
        for rows, lanes in blocks_of(8):
            density, momentum = moments([fbuf[q, rows, lanes] for q in range(Q)])
            mom[0, rows, lanes] = density
            for d in range(3):
                mom[1 + d, rows, lanes] = momentum[d]

    def find_velocity(last):
        for rows, lanes in blocks_of(16):
            density = mom[0, rows, lanes]
            inverse = 1.0 / density
            half = 0.5 * inverse
            for d in range(3):
                moved = mom[1 + d, rows, lanes] * inverse
                value = moved + half * force[d, rows, lanes]
                vel[lanes.start // LANES, pl.ds(d * extent_x + rows.start, 16)] = value.astype(
                    jnp.bfloat16
                )
                if not last:
                    mom[1 + d, rows, lanes] = moved
            if not last:
                mom[0, rows, lanes] = jnp.where(wall[rows, lanes] == 1, 0.0, density)
                scale[rows, lanes] = RELAX_TIME * inverse

    def collide(rg, t, prepared):
        rows = pl.ds(rg * 8, 8)
        lanes = pl.ds(t * LANES, LANES)
        density = mom[0, rows, lanes]
        factor = scale[rows, lanes]
        u = [mom[1 + d, rows, lanes] + factor * force[d, rows, lanes] for d in range(3)]
        square = u[0] * u[0] + u[1] * u[1] + u[2] * u[2]
        part = density * (1.0 - 1.5 * square)
        bases = {w: (gain * w) * part for w in sorted(set(WEIGHTS))}
        twice = {w: (2.0 * gain * w) * density for w in sorted(set(WEIGHTS))}
        half = [1.5 * component for component in u]

        solid = None if prepared else wall[rows, lanes] == 1

        def write(q, own, other, change):
            if prepared:
                rbuf[q, rows, lanes] = own + change
            else:
                rbuf[q, rows, lanes] = jnp.where(solid, other, own * (1.0 - gain) + change)

        f0 = fbuf[0, rows, lanes]
        write(0, f0, f0, bases[WEIGHTS[0]])
        for q in range(1, Q, 2):
            o = OPPOSITE[q]
            along = signed_sum(
                [(LATTICE[q][d], half[d]) for d in range(3) if LATTICE[q][d] != 0]
            )
            fq = fbuf[q, rows, lanes]
            fo = fbuf[o, rows, lanes]
            odd = twice[WEIGHTS[q]] * along
            even = bases[WEIGHTS[q]] + odd * along
            write(q, fq, fo, even + odd)
            write(o, fo, fq, even - odd)

    cell_x = lax.broadcasted_iota(jnp.int32, (extent_x, LANES), 0).astype(jnp.float32)
    cell_y = lax.broadcasted_iota(jnp.int32, (max(8, extent_y), LANES), 0).astype(jnp.float32)
    cell_z = lax.broadcasted_iota(jnp.int32, (NZ, LANES), 0).astype(jnp.float32)

    def hat(coordinate, cells):
        return jnp.maximum(0.0, 1.0 - jnp.abs(coordinate - cells))

    def build(it, k, now, fixed):
        pulls = [SPRING * (fixed[c] - now[c]) for c in range(3)]
        sides, planes = [], []
        for j in range(capacity):
            at = slice(2 * j + 1, 2 * j + 2)
            wx = hat(now[0][at], cell_x)
            wy = hat(now[1][at], cell_y)
            wz = hat(now[2][at], cell_z)
            wxs[it, k * capacity + j] = wx
            flat = jnp.concatenate([wy[y:y + 1] * wz for y in range(extent_y)], axis=0)
            planes.append(flat.astype(jnp.bfloat16))
            side = jnp.concatenate([pulls[c][at] * wx for c in range(3)], axis=0)
            sides.append(side.astype(jnp.bfloat16))
        return jnp.concatenate(sides, axis=1), jnp.concatenate(planes, axis=1)

    def spread(sides, planes):
        return lax.dot_general(
            sides, planes, (((1,), (1,)), ((), ())), preferred_element_type=jnp.float32
        )

    def spread_t(sides, planes):
        field = lax.dot_general(
            planes, sides, (((1,), (1,)), ((), ())), preferred_element_type=jnp.float32
        )
        field = jnp.concatenate([field, jnp.zeros((plane, LANES - 3 * extent_x), jnp.float32)], axis=1)
        return jnp.transpose(field)[0:3 * extent_x]

    def add_force(field, first):
        for d in range(3):
            part = field[d * extent_x:(d + 1) * extent_x]
            force[d] = part if first else force[d] + part

    low_rows = row < 4
    mid_rows = jnp.logical_and(row >= 2, row < 6)
    second = (row & 2) != 0

    def merge(mask, a, b, shift):
        return jnp.where(mask, a, b) + pltpu.roll(jnp.where(mask, b, a), shift, 0)

    def row_sums(parts):
        parts = parts + [jnp.zeros((8, LANES), jnp.float32)] * (4 - len(parts))
        pairs = merge(low_rows, parts[1], parts[3], 4), merge(mid_rows, parts[2], parts[0], 4)
        total = merge(second, pairs[0], pairs[1], 2)
        return total + pltpu.roll(total, 1, 0)

    def move(it, k, planes):
        flow = jnp.concatenate([vel[t] for t in range(tiles)], axis=1)
        sampled = jnp.dot(flow, planes, preferred_element_type=jnp.float32)
        result = []
        for c in range(3):
            parts = []
            for j in range(capacity):
                part = sampled[c * extent_x:(c + 1) * extent_x, j * LANES:(j + 1) * LANES]
                part = part * wxs[it, k * capacity + j]
                parts.append(tree_sum([part[i:i + 8] for i in range(0, extent_x, 8)]))
            result.append(current[k, c] + row_sums(parts))
        return result

    pltpu.make_async_copy(rbuf, rbuf, load_sem.at[2]).wait()
    prepare()
    planes = []
    for k in range(n_xsec):
        if k > 0:
            arrival(arrived, out_sem.at[0], a2a_recv, k).wait_recv()
        now = [arrived[order[k], c] for c in range(3)]
        for c in range(3):
            current[k, c] = now[c]
        sides, flat = build(0, k, now, [pltpu.roll(now[c], 1, 0) for c in range(3)])
        planes.append(flat)
        add_force(spread(sides, flat), k == 0)

    settle_blocks(outgoing, 0)

    depth = lax.broadcasted_iota(jnp.int32, (extent_x, plane), 1) % NZ
    lane = lax.broadcasted_iota(jnp.int32, (extent_x, LANES), 1)
    line = lax.broadcasted_iota(jnp.int32, (1, plane), 1)

    def shift_x(value, step_x, edge):
        rolled = pltpu.roll(value, step_x % extent_x, 0)
        index = lax.broadcasted_iota(jnp.int32, value.shape, 0)
        enters = index == (0 if step_x == 1 else extent_x - 1)
        return jnp.where(enters, jnp.broadcast_to(edge, value.shape), rolled)

    last_tile = pl.ds(plane - LANES, LANES)
    first_tile = pl.ds(0, LANES)

    def halo_rows(it):
        for side, sx in enumerate((1, -1)):
            found = []
            for k, q in enumerate(X_DIRS[sx]):
                _, sy, sz = LATTICE[q]
                amount = sy * NZ + sz
                value = xs_in[it, side, k:k + 1, :]
                if amount != 0:
                    value = pltpu.roll(
                        jnp.broadcast_to(value, (8, plane)), amount % plane, 1
                    )[0:1]
                if sz != 0:
                    value = jnp.where(depth[0:1] == (0 if sz == 1 else NZ - 1), 0.0, value)
                if sy != 0:
                    outside = line < NZ if sy == 1 else line >= plane - NZ
                    value = jnp.where(outside, 0.0, value)
                found.append((q, value))
            yield (0 if sx == 1 else extent_x - 1), found

    def halo_tiles(it):
        for side, sy in enumerate((1, -1)):
            origin = LANES - NZ if sy == 1 else 0
            enters = lane < NZ if sy == 1 else lane >= LANES - NZ
            found = []
            for g, q in enumerate(Y_DIRS[sy]):
                sx, _, sz = LATTICE[q]
                amount = sy * NZ + sz
                finish = origin + amount
                if g < GROUPS:
                    value = pltpu.roll(
                        ys_in[it, side, 0:extent_x, :], (finish - g * NZ) % LANES, 1
                    )
                else:
                    folded = ys_in[it, side, extent_x:extent_x + 8, :]
                    value = jnp.concatenate(
                        [
                            pltpu.roll(folded, (finish - r * NZ) % LANES, 1)
                            for r in range(row_groups)
                        ],
                        axis=0,
                    )
                if sx != 0:
                    corner = pltpu.roll(cs_in[it, CORNERS.index(q)], amount % LANES, 1)
                    value = shift_x(value, sx, corner[7:8] if sx == 1 else corner[0:1])
                keep = enters
                if sz != 0:
                    keep = jnp.logical_and(enters, lane % NZ != (0 if sz == 1 else NZ - 1))
                found.append((q, jnp.where(keep, value, 0.0)))
            yield (first_tile if sy == 1 else last_tile), found

    def add_moments(found, where):
        mom[(0, *where)] = mom[(0, *where)] + tree_sum([value for _, value in found])
        for d in range(3):
            terms = [(LATTICE[q][d], value) for q, value in found if LATTICE[q][d] != 0]
            mom[(1 + d, *where)] = mom[(1 + d, *where)] + signed_sum(
                sorted(terms, key=lambda term: -term[0])
            )

    def halo_values(it):
        return list(halo_rows(it)), list(halo_tiles(it))

    def halo_moments(values):
        for edge, found in values[0]:
            add_moments(found, (slice(edge, edge + 1), slice(None)))
        for tile, found in values[1]:
            add_moments(found, (slice(None), tile))

    def halo_populations(values):
        for edge, found in values[0]:
            for q, value in found:
                fbuf[q, edge:edge + 1, :] = value
        for tile, found in values[1]:
            for q, value in found:
                fbuf[q, :, tile] = fbuf[q, :, tile] + value

    group = lax.broadcasted_iota(jnp.int32, (extent_x, LANES), 1) // NZ
    group8 = lax.broadcasted_iota(jnp.int32, (8, LANES), 1) // NZ
    edge_groups = sorted({0, row_groups - 1})
    side_tiles = {1: tiles - 1, -1: 0}
    stages = {1: [], -1: [], 0: [], None: []}
    for rg in range(row_groups):
        for t in range(tiles):
            if t == side_tiles[1]:
                stages[1].append((rg, t))
            elif t == side_tiles[-1]:
                stages[-1].append((rg, t))
            elif rg in edge_groups:
                stages[0].append((rg, t))
            else:
                stages[None].append((rg, t))

    def corner_copies(it, side):
        for k, q in enumerate(CORNERS):
            sx, sy, _ = LATTICE[q]
            if sy != side:
                continue
            copy = pltpu.make_async_remote_copy(
                src_ref=rbuf.at[
                    q,
                    pl.ds(extent_x - 8 if sx == 1 else 0, 8),
                    last_tile if sy == 1 else first_tile,
                ],
                dst_ref=cs_in.at[it, k],
                send_sem=out_sem.at[0],
                recv_sem=halo_recv.at[it],
                device_id=(v_side[sx], h + sy),
                device_id_type=MESH,
            )
            yield has_side[sy], copy

    def row_copies(it):
        for side, sx in enumerate((1, -1)):
            edge = extent_x - 1 if sx == 1 else 0
            for k, q in enumerate(X_DIRS[sx]):
                xs_out[it, side, k:k + 1, :] = rbuf[q, edge:edge + 1, :]
            yield None, pltpu.make_async_remote_copy(
                src_ref=xs_out.at[it, side],
                dst_ref=xs_in.at[it, side],
                send_sem=out_sem.at[0],
                recv_sem=halo_recv.at[it],
                device_id=(v_side[sx], h),
                device_id_type=MESH,
            )

    def tile_copies(it, sy):
        for side in (0,) if sy == 1 else (1,):
            tile = last_tile if sy == 1 else first_tile
            origin = LANES - NZ if sy == 1 else 0
            dirs = Y_DIRS[sy]
            packed = None
            for g in range(GROUPS):
                part = pltpu.roll(rbuf[dirs[g], :, tile], (g * NZ - origin) % LANES, 1)
                packed = part if packed is None else jnp.where(group == g, part, packed)
            ys_out[it, side, 0:extent_x, :] = packed
            packed = None
            for g in range(row_groups):
                part = pltpu.roll(
                    rbuf[dirs[GROUPS], g * 8:(g + 1) * 8, tile], (g * NZ - origin) % LANES, 1
                )
                packed = part if packed is None else jnp.where(group8 == g, part, packed)
            ys_out[it, side, extent_x:extent_x + 8, :] = packed
            yield has_side[sy], pltpu.make_async_remote_copy(
                src_ref=ys_out.at[it, side],
                dst_ref=ys_in.at[it, side],
                send_sem=out_sem.at[0],
                recv_sem=halo_recv.at[it],
                device_id=(v, h + sy),
                device_id_type=MESH,
            )

    def settle(sem):
        side = row_groups + 1 + len(CORNERS) // 2
        between = jnp.logical_and(has_side[1], has_side[-1])
        most = meter.at[pl.ds(0, 2 * tiles + 2 * side)]
        some = meter.at[pl.ds(0, 2 * tiles + side)]
        pl.when(between)(pltpu.make_async_copy(most, most, sem).wait)
        pl.when(jnp.logical_not(between))(pltpu.make_async_copy(some, some, sem).wait)

    def pass_on():
        for q in range(Q):
            step_x, step_y, step_z = LATTICE[q]
            value = rbuf[q]
            if step_x != 0:
                value = pltpu.roll(value, step_x % extent_x, 0)
            amount = step_y * NZ + step_z
            if amount != 0:
                value = pltpu.roll(value, amount % plane, 1)
            if step_z != 0:
                value = jnp.where(depth == (0 if step_z == 1 else NZ - 1), 0.0, value)
            if step_y != 0:
                column = lax.broadcasted_iota(jnp.int32, (extent_x, plane), 1)
                outside = column < NZ if step_y == 1 else column >= plane - NZ
                value = jnp.where(outside, 0.0, value)
            if step_x != 0:
                index = lax.broadcasted_iota(jnp.int32, (extent_x, plane), 0)
                value = jnp.where(index == (0 if step_x == 1 else extent_x - 1), 0.0, value)
            fbuf[q] = value

    for it in range(ITERS):
        last = it == ITERS - 1

        def send(found):
            for can_send, copy in found:
                if can_send is None:
                    copy.start()
                else:
                    pl.when(can_send)(copy.start)

        for sy in (1, -1):
            for rg, t in stages[sy]:
                collide(rg, t, it == 0)
            send(corner_copies(it, sy))
            send(tile_copies(it, sy))
        for rg, t in stages[0]:
            collide(rg, t, it == 0)
        send(row_copies(it))
        for rg, t in stages[None]:
            collide(rg, t, it == 0)
        pass_on()
        gather_moments()
        settle(halo_recv.at[it])
        values = halo_values(it)
        halo_moments(values)
        find_velocity(last)
        if not last:
            halo_populations(values)
            built = []
            for k in range(n_xsec):
                now = move(it, k, planes[k])
                for c in range(3):
                    current[k, c] = now[c]
                built.append(
                    build(it + 1, k, now, [pltpu.roll(arrived[order[k], c], 1, 0) for c in range(3)])
                )
            planes = [flat for _, flat in built]
            add_force(
                spread(
                    jnp.concatenate([sides for sides, _ in built], axis=1),
                    jnp.concatenate(planes, axis=1),
                ),
                True,
            )
            settle(out_sem.at[0])

    for k in range(n_xsec - 1, -1, -1):
        now = move(ITERS - 1, k, planes[k])
        moved = [now[c] - arrived[order[k], c] for c in range(3)]
        ret_out[k, 0] = jnp.where(odd_row, moved[0], pltpu.roll(moved[1], 7, 0))
        ret_out[k, 1] = moved[2]
        if k > 0:
            transfer(ret_out.at[k], ret_in, out_sem.at[1], ret_recv, k).start()
    halo_populations(halo_values(ITERS - 1))
    settle(out_sem.at[0])
    settle_blocks(ret_out, 1)
    totals = [jnp.zeros((8, LANES), jnp.float32) for _ in range(3)]
    for k in range(n_xsec):
        if k > 0:
            arrival(ret_in, out_sem.at[1], ret_recv, k).wait_recv()
        found = [ret_out[0, i] if k == 0 else ret_in[order[k], i] for i in range(2)]
        for j in range(capacity):
            here = place == order[k] * capacity + j
            for c in range(3):
                at = 2 * j + (0 if c == 1 else 1)
                value = found[c // 2][at:at + 1]
                totals[c] = jnp.where(here, spread_row(value), totals[c])
    for c in range(3):
        disp[c] = totals[c][0:owned]


CHUNKS = 1


def hand_over(evolved_in, moved_in, evolved, moved, out_sem):
    size = -(-Q // CHUNKS)
    stores = [pltpu.make_async_copy(moved_in, moved, out_sem.at[CHUNKS])]
    for i, first in enumerate(range(0, Q, size)):
        part = pl.ds(first, min(size, Q - first))
        stores.append(
            pltpu.make_async_copy(evolved_in.at[part], evolved.at[part], out_sem.at[i])
        )
    for store in stores:
        store.start()
    for store in stores:
        store.wait()


def per_device(n_vessel, n_xsec, populations, wall_flags, positions, vertex_rest_shift, home_brick):
    owned = positions.shape[0]
    capacity = max(2, 2 * owned // n_xsec)
    slots = n_xsec * capacity
    extent_x, plane = populations.shape[1:]
    f32 = jnp.float32
    meters = 2 * (plane // LANES + extent_x // 8 + 1) + len(CORNERS)
    vmem = pl.BlockSpec(memory_space=pltpu.VMEM)
    hbm = pl.BlockSpec(memory_space=pltpu.HBM)
    dma = pltpu.SemaphoreType.DMA
    evolved, moved = pl.pallas_call(
        functools.partial(kernel, n_vessel, n_xsec, capacity, extent_x, plane),
        out_shape=(
            pltpu.VMEM(populations.shape, f32),
            pltpu.VMEM((3, owned, LANES), f32),
        ),
        in_specs=[hbm] * 5,
        out_specs=(vmem, vmem),
        scratch_shapes=[
            pltpu.VMEM((extent_x, plane), jnp.int32),
            pltpu.VMEM((2, 3, owned, LANES), f32),
            pltpu.SMEM((1, owned), jnp.int32),
            pltpu.VMEM((Q + 1, extent_x, plane), f32),
            pltpu.VMEM((4, extent_x, plane), f32),
            pltpu.VMEM((extent_x, plane), f32),
            pltpu.VMEM((3, extent_x, plane), f32),
            pltpu.VMEM((plane // LANES, 3 * extent_x, LANES), jnp.bfloat16),
            pltpu.VMEM((n_xsec, 3, 8, LANES), f32),
            pltpu.VMEM((n_xsec, 3, 8, LANES), f32),
            pltpu.VMEM((n_xsec, 3, 8, LANES), f32),
            pltpu.VMEM((n_xsec, 2, 8, LANES), f32),
            pltpu.VMEM((n_xsec, 2, 8, LANES), f32),
            pltpu.VMEM((ITERS, slots, extent_x, LANES), f32),
            pltpu.VMEM((ITERS, 2, 8, plane), f32),
            pltpu.VMEM((ITERS, 2, 8, plane), f32),
            pltpu.VMEM((ITERS, 2, extent_x + 8, LANES), f32),
            pltpu.VMEM((ITERS, 2, extent_x + 8, LANES), f32),
            pltpu.VMEM((ITERS, len(CORNERS), 8, LANES), f32),
            pltpu.VMEM((meters, 8, LANES), f32),
            dma((3,)),
            dma((2,)),
            dma((n_xsec - 1,)),
            dma((n_xsec - 1,)),
            dma((ITERS,)),
        ],
        compiler_params=pltpu.CompilerParams(
            collective_id=0, has_side_effects=True, vmem_limit_bytes=40 << 20
        ),
    )(
        *(
            pltpu.with_memory_space_constraint(value, pltpu.HBM)
            for value in (
                populations,
                wall_flags,
                jnp.transpose(positions, (1, 0, 2)),
                jnp.transpose(vertex_rest_shift, (1, 0, 2)),
                jnp.transpose(home_brick),
            )
        )
    )
    evolved, moved = pl.pallas_call(
        hand_over,
        out_shape=(
            jax.ShapeDtypeStruct(evolved.shape, f32),
            jax.ShapeDtypeStruct(moved.shape, f32),
        ),
        in_specs=[vmem, vmem],
        out_specs=(hbm, hbm),
        scratch_shapes=[dma((CHUNKS + 1,))],
        compiler_params=pltpu.CompilerParams(vmem_limit_bytes=1 << 20),
    )(
        pltpu.with_memory_space_constraint(evolved, pltpu.VMEM),
        pltpu.with_memory_space_constraint(moved, pltpu.VMEM),
    )
    return evolved, jnp.transpose(moved, (1, 0, 2))


def solution(mesh):
    in_specs = (
        P(None, "vessel", "xsec"),
        P("vessel", "xsec"),
        P(("vessel", "xsec"), None, None),
        P(("vessel", "xsec"), None, None),
        P(("vessel", "xsec"), None),
    )
    out_specs = (P(None, "vessel", "xsec"), P(("vessel", "xsec"), None, None))
    return jax.shard_map(
        functools.partial(per_device, mesh.shape["vessel"], mesh.shape["xsec"]),
        mesh=mesh,
        in_specs=in_specs,
        out_specs=out_specs,
        check_vma=False,
    )
```
